128 devices in a mesh: side: 2 (over core), row: 4 (over x), col: 16 (over y, z).
Axes of the slice: x: 4, y: 4, z: 4, core: 2. Of those that a mesh axis runs over, the one named last changes fastest.
Arguments:
- right_side: float32 [256, 512, 548], P('row', 'col', 'side'), may hold values from -24 to 24
- couplings: float32 [4, 256, 512], P(None, 'row', 'col'), may hold values from 0.04 to 0.2
- channel_rates: float32 [548], P('side'), may hold values from 0.2 to 1
- weight_in: float32 [548, 1024], replicated, may hold values from -0.25 to 0.25
- weight_mid: float32 [1024, 1024], replicated, may hold values from -0.1875 to 0.1875
- weight_out: float32 [1024, 616], replicated, may hold values from -0.1875 to 0.1875
- inverse_cov: float32 [616, 616], replicated, may hold values from -2 to 8, as said below
- profile_cells: int32 [2, 32768], P(None, ('row', 'col')), may hold values from 0 to 2047
- profile_counts: int32 [128], replicated, may hold values from 1 to 512, 16384 in all
- gate_first: bfloat16 [65536, 1024], P(('side', 'row', 'col')), may hold values from 0 to 1.09375
- gate_second: bfloat16 [65536, 1024], P(('side', 'row', 'col')), may hold values from 0 to 1.09375
Outputs:
- solution: float32 [256, 512, 548], P('row', 'col', 'side')
- residual: float32 [256, 512, 548], P('row', 'col', 'side')
The draws below stay inside these ranges and needn't reach their ends.
Inputs may be any that keep to these rules, and one draw needn't show every extreme that they name: `profile_counts`: entry d counts the live profiles of device d in the order side, row, col; they fill its first slots. The entries add up to 16384, and the largest is 512. `profile_cells`: entry [s, t * 512 + i] is the cell, numbered latitude-major within tile t, observed by slot i of device s * 64 + t; entries of slots that are not live are unused. `inverse_cov`: symmetric positive definite.
All inputs are finite; a program needn't handle non-finite values.
Results may differ from the reference program's by a relative error of at most 0.0003.
Values may be sent and summed in bfloat16 or wider, within the bound.
No kernel may reach another device: no remote copies, remote signals or barrier semaphores. Data moves between devices by JAX's collectives and lax.ppermute only.
A program may use at most 128 MiB of HBM per device.

```python
import math
import jax
import jax.numpy as jnp
import numpy as np
from jax import lax

CLAT = 64
CLON = 32
NVAL = 548
HID = 1024
NOUT = 616
BAL = 128
ITERS = 2
PSLOT = 512
CELLS = 2048
TILES = 64
NLAT = 256
NLON = 512
PROFILES = 65536
N_SIDE = 2
N_COL = 16
DEVICES = 128


def draw_right_side(key, part):
    latitude = jnp.arange(NLAT, dtype=jnp.float32)[:, None, None] / NLAT
    longitude = jnp.arange(NLON, dtype=jnp.float32)[None, :, None] / NLON
    channel = jnp.arange(NVAL, dtype=jnp.float32)[None, None, :] / NVAL
    spread_scale = jnp.exp(0.5 * jnp.log(3.0) * (latitude + longitude + channel))
    random_part = jnp.clip(jax.random.normal(key, (NLAT, NLON, NVAL), jnp.float32), -4.0, 4.0)
    return random_part * spread_scale


def draw_inverse_cov(key, part):
    diag_key = jax.random.fold_in(key, 11)
    matrix_key = jax.random.fold_in(key, 23)
    diagonal = 1.0 + 2.0 * jax.random.uniform(diag_key, (NOUT,), jnp.float32)
    random_matrix = jnp.clip(jax.random.normal(matrix_key, (NOUT, NOUT), jnp.float32), -4.0, 4.0)
    product_part = jnp.dot(random_matrix, random_matrix.T, precision=lax.Precision.HIGHEST) / NOUT
    product_part = 0.5 * (product_part + product_part.T)
    return product_part + jnp.diag(diagonal)


def touch_ends(entries, rng, least, high):
    spot = [jax.random.randint(jax.random.fold_in(rng, axis), (), 0, length) for axis, length in enumerate(entries.shape)]
    main_axis = entries.shape.index(max(entries.shape))
    neighbour = spot[:main_axis] + [(spot[main_axis] + 1) % entries.shape[main_axis]] + spot[main_axis + 1:]
    return entries.at[tuple(spot)].set(least).at[tuple(neighbour)].set(high)


def shard_levels(stream_key, dims, split, low, largest):
    level, own = 1.0, jax.random.fold_in(stream_key, 6)
    for position, parts in split:
        steps = jnp.exp(jax.random.uniform(jax.random.fold_in(own, position), (parts,), jnp.float32, low / len(split), largest / len(split)))
        level = level * jnp.repeat(steps, dims[position] // parts).reshape([-1 if axis == position else 1 for axis in range(len(dims))])
    return level


def length_profile(number_of, total, most, slope):
    loads = [(1 << 20) // math.isqrt(standing ** slope) + 1 for standing in range(2, number_of + 1)]
    spare, given = total - most - (number_of - 1), [1] * (number_of - 1)
    while spare > 0:
        free = [i for i in range(number_of - 1) if given[i] < most]
        pool, remaining = sum([loads[i] for i in free]), spare
        for i in free:
            addition = min(most - given[i], max(1, remaining * loads[i] // pool), spare)
            given[i] = given[i] + addition
            spare = spare - addition
    return np.array([most] + given)


def ragged(rng, count, total, reach, skew):
    if count == 2:
        one = jax.random.randint(rng, (), max(1, total - reach), min(reach, total - 1) + 1)
        return jnp.stack([one, total - one])
    tallies = jnp.asarray(length_profile(count, total, reach, skew), jnp.int32)
    twos = (count - 1) // 2
    source_of, taker = tallies[1:1 + 2 * twos:2], tallies[2:2 + 2 * twos:2]
    slack = jnp.minimum(source_of - 1, reach - taker)
    moved = jax.random.randint(jax.random.fold_in(rng, 1), (twos,), 0, 1 << 20) % (slack + 1)
    tallies = tallies.at[1:1 + 2 * twos:2].set(source_of - moved).at[2:2 + 2 * twos:2].set(taker + moved)
    return tallies[jax.random.permutation(jax.random.fold_in(rng, 2), count)]


def scatter_about(stream_key, shape, deviation, reach, kind=jnp.bfloat16):
    values = deviation * jax.random.normal(stream_key, shape, jnp.float32)
    return jnp.clip(values, min=-reach, max=reach).astype(kind)


def setup_inputs(seed: int = 0) -> dict:
    key_list = jax.random.split(jax.random.key(seed), 12)
    return {
        "right_side": draw_right_side(jax.random.fold_in(key_list[11], 71), 0),
        "couplings": jnp.clip(jnp.exp(math.log(0.2) - 1.609438 * jax.random.uniform(key_list[1], (4, NLAT, NLON), jnp.float32) ** shard_levels(key_list[1], (4, NLAT, NLON), ((1, 4), (2, 16)), -0.2, 0.2)), 0.04, 0.2),
        "channel_rates": jnp.clip(jnp.exp(math.log(1.0) - 1.609438 * jax.random.uniform(key_list[2], (NVAL,), jnp.float32) ** shard_levels(key_list[2], (NVAL,), ((0, 2),), -0.2, 0.2)), 0.2, 1.0),
        "weight_in": scatter_about(key_list[3], (NVAL, HID), NVAL ** -0.5, 0.25, jnp.float32),
        "weight_mid": scatter_about(key_list[4], (HID, HID), HID ** -0.5, 0.1875, jnp.float32),
        "weight_out": scatter_about(key_list[5], (HID, NOUT), HID ** -0.5, 0.1875, jnp.float32),
        "inverse_cov": draw_inverse_cov(jax.random.fold_in(key_list[11], 71), 0),
        "profile_cells": touch_ends(jax.random.randint(key_list[7], (N_SIDE, TILES * PSLOT), 0, CELLS), jax.random.fold_in(key_list[7], 1), 0, CELLS - 1).astype(jnp.int32),
        "profile_counts": ragged(key_list[8], DEVICES, DEVICES * BAL, PSLOT, 2).astype(jnp.int32),
        "gate_first": jnp.clip(1.09375 * jax.random.uniform(key_list[9], (PROFILES, HID), jnp.float32) ** shard_levels(key_list[9], (PROFILES, HID), ((0, 128),), -0.2, 0.2), 0.0, 1.09375).astype(jnp.bfloat16),
        "gate_second": jnp.clip(1.09375 * jax.random.uniform(key_list[10], (PROFILES, HID), jnp.float32) ** shard_levels(key_list[10], (PROFILES, HID), ((0, 128),), -0.2, 0.2), 0.0, 1.09375).astype(jnp.bfloat16),
    }


highest = lax.Precision.HIGHEST


def product(first_matrix, second_matrix):
    return jnp.dot(first_matrix, second_matrix, precision=highest, preferred_element_type=jnp.float32)


def product_back(first_matrix, second_matrix):
    return lax.dot_general(first_matrix, second_matrix, (((1,), (1,)), ((), ())), precision=highest, preferred_element_type=jnp.float32)


def network(profile_rows, gate_one, gate_two, weight_in, weight_mid, weight_out, inverse_cov):
    hidden = product(profile_rows, weight_in) * gate_one
    hidden = product(hidden, weight_mid) * gate_two
    weighted = product(product(hidden, weight_out), inverse_cov)
    adjoint_part = product_back(weighted, weight_out) * gate_two
    adjoint_part = product_back(adjoint_part, weight_mid) * gate_one
    return product_back(adjoint_part, weight_in)


def masked_couplings(couplings):
    latitude = jnp.arange(NLAT)[:, None]
    north_part = jnp.where(latitude < NLAT - 1, couplings[2], 0.0)
    south_part = jnp.where(latitude > 0, couplings[3], 0.0)
    return couplings[0], couplings[1], north_part, south_part


def tangent(state_field, weights, channel_rates):
    east_weight, west_weight, north_weight, south_weight = weights
    net_flux = east_weight[:, :, None] * (jnp.roll(state_field, -1, axis=1) - state_field)
    net_flux = net_flux + west_weight[:, :, None] * (jnp.roll(state_field, 1, axis=1) - state_field)
    net_flux = net_flux + north_weight[:, :, None] * (jnp.roll(state_field, -1, axis=0) - state_field)
    net_flux = net_flux + south_weight[:, :, None] * (jnp.roll(state_field, 1, axis=0) - state_field)
    return state_field + channel_rates * net_flux


def adjoint(state_field, weights, channel_rates):
    east_weight, west_weight, north_weight, south_weight = weights
    scaled = channel_rates * state_field
    coupling_sum = (east_weight + west_weight + north_weight + south_weight)[:, :, None]
    result = state_field - coupling_sum * scaled
    result = result + jnp.roll(east_weight[:, :, None] * scaled, 1, axis=1)
    result = result + jnp.roll(west_weight[:, :, None] * scaled, -1, axis=1)
    result = result + jnp.roll(north_weight[:, :, None] * scaled, 1, axis=0)
    result = result + jnp.roll(south_weight[:, :, None] * scaled, -1, axis=0)
    return result


def observe(model_image, profile_cells, profile_counts, gate_first, gate_second, weight_in, weight_mid, weight_out, inverse_cov):
    count_ends = jnp.cumsum(profile_counts).astype(jnp.int32)
    starts = (count_ends - profile_counts).astype(jnp.int32)
    global_rank = jnp.arange(DEVICES * BAL, dtype=jnp.int32)
    source = jnp.searchsorted(count_ends, global_rank, side="right").astype(jnp.int32)
    local_row = (global_rank - starts[source]).astype(jnp.int32)
    side_index = source // TILES
    tile_index = source % TILES
    cell_index = profile_cells[side_index, tile_index * PSLOT + local_row].astype(jnp.int32)
    latitude = (tile_index // N_COL) * CLAT + cell_index // CLON
    longitude = (tile_index % N_COL) * CLON + cell_index % CLON
    flat_cell = (latitude * NLON + longitude).astype(jnp.int32)
    slot_index = (source * PSLOT + local_row).astype(jnp.int32)
    columns = model_image.reshape(NLAT * NLON, NVAL)[flat_cell]
    block_rows = min(1024, DEVICES * BAL)

    def run_block(pieces):
        return network(pieces[0], pieces[1], pieces[2], weight_in, weight_mid, weight_out, inverse_cov)

    gradients = lax.map(run_block, (columns.reshape(-1, block_rows, NVAL), gate_first[slot_index].reshape(-1, block_rows, HID), gate_second[slot_index].reshape(-1, block_rows, HID)))
    summed = jax.ops.segment_sum(gradients.reshape(-1, NVAL), flat_cell, num_segments=NLAT * NLON)
    return summed.reshape(NLAT, NLON, NVAL)


def reference(right_side, couplings, channel_rates, weight_in, weight_mid, weight_out, inverse_cov, profile_cells, profile_counts, gate_first, gate_second):
    weights = masked_couplings(couplings)

    def hessian(direction):
        model_image = tangent(direction, weights, channel_rates)
        spread_field = observe(model_image, profile_cells, profile_counts, gate_first, gate_second, weight_in, weight_mid, weight_out, inverse_cov)
        return direction + adjoint(spread_field, weights, channel_rates)

    solution = jnp.zeros_like(right_side)
    residual = right_side
    direction = right_side
    norm_now = jnp.sum(residual * residual)
    for iteration in range(ITERS):
        hessian_image = hessian(direction)
        step_size = norm_now / jnp.sum(direction * hessian_image)
        solution = solution + step_size * direction
        residual = residual - step_size * hessian_image
        if iteration + 1 < ITERS:
            norm_next = jnp.sum(residual * residual)
            direction = residual + (norm_next / norm_now) * direction
            norm_now = norm_next
    return solution, residual
```

```python
import jax
import jax.numpy as jnp
from jax import lax
from jax.sharding import PartitionSpec as P

SCALE = 2.0**40
high = lax.Precision.HIGH


def product(first_matrix, second_matrix):
    return jnp.dot(first_matrix, second_matrix, precision=high, preferred_element_type=jnp.float32)


def product_back(first_matrix, second_matrix):
    return lax.dot_general(
        first_matrix,
        second_matrix,
        (((1,), (1,)), ((), ())),
        precision=high,
        preferred_element_type=jnp.float32,
    )


def shifted(value, axis, step):
    count = lax.axis_size(axis)
    return lax.ppermute(value, axis, [(i, (i + step) % count) for i in range(count)])


def halos(south_row, north_row, west_col, east_col):
    from_south = shifted(north_row, "row", 1)
    from_north = shifted(south_row, "row", -1)
    from_west = shifted(east_col, "col", 1)
    from_east = shifted(west_col, "col", -1)
    return from_south, from_north, from_west, from_east


def edges(field):
    return field[:1], field[-1:], field[:, :1], field[:, -1:]


def stencil_parts(field, around):
    from_south, from_north, from_west, from_east = around
    east = jnp.concatenate([field[:, 1:], from_east], axis=1)
    west = jnp.concatenate([from_west, field[:, :-1]], axis=1)
    north = jnp.concatenate([field[1:], from_north], axis=0)
    south = jnp.concatenate([from_south, field[:-1]], axis=0)
    return east, west, north, south


def tangent(field, weights, channel_rates):
    east, west, north, south = stencil_parts(field, halos(*edges(field)))
    flux = weights[0][:, :, None] * (east - field)
    flux = flux + weights[1][:, :, None] * (west - field)
    flux = flux + weights[2][:, :, None] * (north - field)
    flux = flux + weights[3][:, :, None] * (south - field)
    return field + channel_rates * flux


def swapped(value):
    return lax.ppermute(value, "side", [(0, 1), (1, 0)])


def everyone(values):
    n = 4
    total = values + swapped(values)
    total = total + sum(shifted(total, "row", k) for k in range(1, n))
    size = lax.axis_size("col")
    for group in ("low", "high"):
        base = total
        for k in range(1, n):
            if group == "low":
                pairs = [(c, (c // n) * n + (c % n + k) % n) for c in range(size)]
            else:
                pairs = [(c, ((c // n + k) % n) * n + c % n) for c in range(size)]
            total = total + lax.ppermute(base, "col", pairs)
    return total


def local(
    right_side,
    couplings,
    channel_rates,
    weight_in,
    weight_mid,
    weight_out,
    inverse_cov,
    profile_cells,
    profile_counts,
    gate_first,
    gate_second,
):
    side_index = lax.axis_index("side")
    tile_count = lax.axis_size("row") * lax.axis_size("col")
    tile_index = lax.axis_index("row") * lax.axis_size("col") + lax.axis_index("col")
    lat_rows, lon_cols, half_width = right_side.shape
    slot_count = profile_cells.shape[1]
    latitude = lax.axis_index("row") * lat_rows + jnp.arange(lat_rows)
    north_open = (latitude < lat_rows * lax.axis_size("row") - 1)[:, None]
    south_open = (latitude > 0)[:, None]
    weights = (
        couplings[0],
        couplings[1],
        jnp.where(north_open, couplings[2], 0.0),
        jnp.where(south_open, couplings[3], 0.0),
    )
    pair_counts = jnp.stack([profile_counts[tile_index], profile_counts[tile_count + tile_index]])
    live_mask = (jnp.arange(slot_count)[None, :] < pair_counts[:, None])[:, :, None]
    own_live = lax.dynamic_index_in_dim(live_mask, side_index, 0, keepdims=False)
    flat_cells = profile_cells.reshape(-1)
    lower_first = side_index == 0

    def observe(field):
        image = tangent(field, weights, channel_rates)
        flat_image = image.reshape(lat_rows * lon_cols, half_width)
        halves = jnp.where(live_mask, flat_image[flat_cells].reshape(2, slot_count, half_width), 0.0)
        own_half = lax.dynamic_index_in_dim(halves, side_index, 0, keepdims=False)
        other_half = lax.dynamic_index_in_dim(halves, 1 - side_index, 0, keepdims=False)
        partner_half = swapped(other_half)
        rows = jnp.where(
            lower_first,
            jnp.concatenate([own_half, partner_half], axis=1),
            jnp.concatenate([partner_half, own_half], axis=1),
        )
        hidden = product(rows, weight_in) * gate_first
        hidden = product(hidden, weight_mid) * gate_second
        outputs = product(hidden, weight_out)
        weighted = product(outputs, inverse_cov)
        quadratic = jnp.sum(jnp.where(own_live, outputs * weighted, 0.0))
        back = product_back(weighted, weight_out) * gate_second
        back = product_back(back, weight_mid) * gate_first
        gradients = product_back(back, weight_in)
        first_half = gradients[:, :half_width]
        second_half = gradients[:, half_width:]
        own_grad = jnp.where(lower_first, first_half, second_half)
        other_grad = jnp.where(lower_first, second_half, first_half)
        partner_grad = swapped(other_grad)
        pair_grads = jnp.where(
            lower_first, jnp.stack([own_grad, partner_grad]), jnp.stack([partner_grad, own_grad])
        )
        return pair_grads, quadratic

    def spread(pair_grads):
        summed = jax.ops.segment_sum(
            pair_grads.reshape(-1, half_width), flat_cells, num_segments=lat_rows * lon_cols
        ).reshape(lat_rows, lon_cols, half_width)
        scaled = channel_rates * summed
        south_row, north_row, west_col, east_col = edges(scaled)
        around = halos(
            weights[3][:1, :, None] * south_row,
            weights[2][-1:, :, None] * north_row,
            weights[1][:, :1, None] * west_col,
            weights[0][:, -1:, None] * east_col,
        )
        total = (weights[0] + weights[1] + weights[2] + weights[3])[:, :, None]
        result = summed - total * scaled
        from_south, from_north, from_west, from_east = around
        flux = [w[:, :, None] * scaled for w in weights]
        result = result + jnp.concatenate([from_west, flux[0][:, :-1]], axis=1)
        result = result + jnp.concatenate([flux[1][:, 1:], from_east], axis=1)
        result = result + jnp.concatenate([from_south, flux[2][:-1]], axis=0)
        result = result + jnp.concatenate([flux[3][1:], from_north], axis=0)
        return result

    grads, _ = observe(right_side)
    basis = spread(grads * (1.0 / SCALE))
    grads, quadratic = observe(basis)
    sums = everyone(
        jnp.stack(
            [
                jnp.sum(right_side * right_side),
                jnp.sum(right_side * basis),
                jnp.sum(basis * basis),
                quadratic,
            ]
        )
    )
    image = spread(grads)
    rr, rv, vv, vy = sums[0], sums[1], sums[2], sums[3]
    q = SCALE * rv
    den = rr + q
    first_step = rr / den
    p = SCALE * first_step
    rest = q / den
    new = p * p * vv - rest * rest * rr
    a = rest + new / rr
    square = a * a * rr - 2.0 * a * p * rv + p * p * vv
    curve = a * a * q - 2.0 * a * p * (SCALE * vv) + p * p * vy
    step = new / (square + curve)
    solution = (first_step + step * a) * right_side - (step * p) * basis
    residual = (
        (rest - step * a) * right_side
        + (step * p - p - step * a * SCALE) * basis
        + (step * p) * image
    )
    return (solution, residual)


def solution(mesh):
    in_specs = (
        P("row", "col", "side"),
        P(None, "row", "col"),
        P("side"),
        P(),
        P(),
        P(),
        P(),
        P(None, ("row", "col")),
        P(),
        P(("side", "row", "col"), None),
        P(("side", "row", "col"), None),
    )
    out_specs = (P("row", "col", "side"), P("row", "col", "side"))
    return jax.shard_map(local, mesh=mesh, in_specs=in_specs, out_specs=out_specs, check_vma=False)
```

```python
import functools

import jax
import jax.numpy as jnp
from jax import lax
from jax.experimental import pallas as pl
from jax.experimental.pallas import tpu as pltpu
from jax.sharding import PartitionSpec as P

SCALE = 2.0**40
BLOCK = 256
f32, bf16 = jnp.float32, jnp.bfloat16
vmem = pl.BlockSpec(memory_space=pltpu.VMEM)
smem = pl.BlockSpec(memory_space=pltpu.SMEM)
hbm = pl.BlockSpec(memory_space=pl.ANY)


WIDE = 384
GROUP = 4


def shape(dims, dtype=f32):
    return jax.ShapeDtypeStruct(dims, dtype)


def call(kernel, out, in_specs, out_specs, scratch, mib, micros):
    return pl.pallas_call(
        kernel,
        out_shape=out,
        in_specs=in_specs,
        out_specs=out_specs,
        scratch_shapes=scratch,
        compiler_params=pltpu.CompilerParams(vmem_limit_bytes=mib << 20),
        cost_estimate=pl.CostEstimate(
            flops=int(micros * 1e9), bytes_accessed=int(micros * 3e6), transcendentals=0
        ),
    )


def halves_of(value):
    upper = value.astype(bf16)
    return upper, (value - upper.astype(f32)).astype(bf16)


def folded(value):
    rows, width = value.shape
    return jnp.sum(value.reshape(rows // 8, 8, width), axis=0)


def lane_vector(scalars):
    lane = lax.broadcasted_iota(jnp.int32, (8, 128), 1)
    result = jnp.zeros((8, 128), f32)
    for k, value in enumerate(scalars):
        result = jnp.where(lane == k, value, result)
    return result


def from_west(value, west_row, lon):
    last = value.shape[0] - 1
    return jnp.where(lon == 0, west_row, jnp.concatenate([value[last:], value[:last]], axis=0))


def from_east(value, east_row, lon):
    last = value.shape[0] - 1
    return jnp.where(lon == last, east_row, jnp.concatenate([value[1:], value[:1]], axis=0))


def sweep(lats, row, below, above, south, north, carry, after=None):
    def group(g, low, high, carry):
        for k in range(GROUP):
            i = g * GROUP + k
            under = south if low and k == 0 else below(i)
            over = north if high and k == GROUP - 1 else above(i)
            carry = row(i, under, over, carry)
        if after is not None:
            after(g)
        return carry

    last = lats // GROUP - 1
    carry = group(0, True, False, carry)
    carry = lax.fori_loop(1, last, lambda g, c: group(g, False, False, c), carry)
    return group(last, False, True, carry)


def prepare_kernel(
    side, w_in, w_mid, w_out, cov, in_hi, in_lo, mid_hi, mid_lo, out_hi, out_lo, cov_hi, cov_lo,
    s_in, s_cov, s_out, s_mid, sems
):
    sources = ((w_in, s_in), (cov, s_cov), (w_out, s_out), (w_mid, s_mid))
    copies = [pltpu.make_async_copy(a, b, sems.at[k]) for k, (a, b) in enumerate(sources)]
    for copy in copies:
        copy.start()
    for target in (in_hi, in_lo, out_hi, out_lo, cov_hi, cov_lo):
        target[...] = jnp.zeros_like(target)
    half = w_in.shape[0] // 2
    hidden = w_mid.shape[0]
    channels = cov.shape[0]

    def columns(total, step, move):
        def body(k, carry):
            move(pl.ds(pl.multiple_of(k * step, step), step))
            return carry

        lax.fori_loop(0, total // step, body, 0)
        if total % step:
            move(slice(total - total % step, total))

    copies[0].wait()
    for flag in range(2):

        @pl.when(side[0] == flag)
        def _(flag=flag):
            for target, source in ((0, flag * half), (WIDE, (1 - flag) * half)):

                def move(n, target=target, source=source):
                    upper, lower = halves_of(s_in[source : source + half, n])
                    in_hi[target : target + half, n] = upper
                    in_lo[target : target + half, n] = lower

                columns(hidden, 128, move)

    copies[1].wait()

    def move_cov(n):
        upper, lower = halves_of(s_cov[:, n])
        cov_hi[:channels, n] = upper
        cov_lo[:channels, n] = lower

    columns(channels, 128, move_cov)
    copies[2].wait()

    def move_out(n):
        upper, lower = halves_of(s_out[:, n])
        out_hi[:channels, n] = upper
        out_lo[:channels, n] = lower

    columns(hidden, 128, move_out)
    copies[3].wait()

    def move_mid(n):
        upper, lower = halves_of(s_mid[n, :])
        mid_hi[n, :] = upper
        mid_lo[n, :] = lower

    columns(hidden, 64, move_mid)


def prepare_call(side, w_in, w_mid, w_out, cov, channels):
    hidden = w_mid.shape[0]
    dims = [(2 * WIDE, hidden), (hidden, hidden), (channels, hidden), (channels, channels)]
    out = [shape(d, bf16) for d in dims for _ in range(2)]
    return call(
        prepare_kernel,
        out,
        [smem] + [hbm] * 4,
        [vmem] * 8,
        [pltpu.VMEM(m.shape, f32) for m in (w_in, cov, w_out, w_mid)]
        + [pltpu.SemaphoreType.DMA((4,))],
        16,
        5,
    )(side, w_in, w_mid, w_out, cov)


def tangent_kernel(
    with_square, cells, counts, field, south, north, west, east, coupling, rates, own, other, *rest
):
    image = rest[-1]
    lats, lons, width = field.shape
    rate = rates[...]
    tail = width - 256
    lon = lax.broadcasted_iota(jnp.int32, (lons, width), 0)
    image[2] = jnp.zeros_like(image[2])

    def row(i, below, above, total):
        value = field[i]
        c = coupling[i]
        to_west = from_west(value, west[pl.ds(i, 1), :], lon)
        to_east = from_east(value, east[pl.ds(i, 1), :], lon)
        flux = c[:, 0:1] * (to_east - value)
        flux = flux + c[:, 1:2] * (to_west - value)
        flux = flux + c[:, 2:3] * (above - value)
        flux = flux + c[:, 3:4] * (below - value)
        result = value + rate * flux
        rows = pl.ds(i * lons if isinstance(i, int) else pl.multiple_of(i * lons, lons), lons)
        image[0, rows, :] = result[:, 0:128]
        image[1, rows, :] = result[:, 128:256]
        image[2, rows, 0:tail] = result[:, 256:]
        if with_square:
            total = total + folded(value * value)
        return total

    total = jnp.zeros((8, width), f32)
    total = sweep(
        lats, row, lambda i: field[i - 1], lambda i: field[i + 1], south[0], north[0], total
    )
    if with_square:
        rest[0][...] = lane_vector([jnp.sum(total)])

    def gather(which, out):
        def body(b, carry):
            first = pl.multiple_of(b * 8, 8)
            found = [cells[which, first + k] for k in range(8)]
            rows = [[image[t, pl.ds(cell, 1), :] for t in range(3)] for cell in found]
            for k in range(8):
                out[pl.ds(first + k, 1), :] = jnp.concatenate(rows[k], axis=1)
            return carry

        lax.fori_loop(0, (counts[which] + 7) // 8, body, 0)

    gather(1, other)
    gather(0, own)


def tangent_call(with_square, cells, counts, field, halo, coupling, rates):
    lats, lons, width = field.shape
    slots = cells.shape[1]
    out = [shape((slots, WIDE))] * 2 + [shape((8, 128))] * with_square
    return call(
        functools.partial(tangent_kernel, with_square),
        out,
        [smem, smem] + [vmem] * 7,
        [vmem] * len(out),
        [pltpu.VMEM((3, lats * lons, 128), f32)],
        8,
        6,
    )(cells, counts, field, *halo, coupling, rates)


def tile(left, right, n, transposed):
    hi, lo = left
    if transposed:
        pick = [w[pl.ds(n, BLOCK), :] for w in right]
        dims = (((1,), (1,)), ((), ()))
    else:
        pick = [w[:, pl.ds(n, BLOCK)] for w in right]
        dims = (((1,), (0,)), ((), ()))
    dot = functools.partial(lax.dot_general, dimension_numbers=dims, preferred_element_type=f32)
    upper = hi[...]
    return dot(upper, pick[0]) + dot(upper, pick[1]) + dot(lo[...], pick[0])


def layer(left, right, columns, transposed, finish, carry=0):
    def body(k, carry):
        n = pl.multiple_of(k * BLOCK, BLOCK)
        return finish(n, tile(left, right, n, transposed), carry)

    return lax.fori_loop(0, columns // BLOCK, body, carry)


def gated(gate, target):
    def finish(n, value, carry):
        upper, lower = halves_of(value * gate[:, pl.ds(n, BLOCK)].astype(f32))
        target[0][:, pl.ds(n, BLOCK)] = upper
        target[1][:, pl.ds(n, BLOCK)] = lower
        return carry

    return finish


def forward_kernel(
    with_sums, counts, own, other, gate_one, gate_two,
    in_hi, in_lo, mid_hi, mid_lo, out_hi, out_lo, cov_hi, cov_lo, *rest
):
    if with_sums:
        sums_in, z_hi, z_lo, sums = rest[:4]
    else:
        z_hi, z_lo = rest[:2]
    x_hi, x_lo, a_hi, a_lo, b_hi, b_lo, t_full, t_hi, t_lo = rest[-9:]
    rows = own.shape[0]
    for start, part in ((0, own), (WIDE, other)):
        upper, lower = halves_of(part[...])
        x_hi[:, start : start + WIDE] = upper
        x_lo[:, start : start + WIDE] = lower
    hidden = mid_hi.shape[0]
    channels = cov_hi.shape[0]
    layer((x_hi, x_lo), (in_hi, in_lo), hidden, False, gated(gate_one, (a_hi, a_lo)))
    layer((a_hi, a_lo), (mid_hi, mid_lo), hidden, False, gated(gate_two, (b_hi, b_lo)))

    def keep_outputs(n, value, carry):
        if with_sums:
            t_full[:, pl.ds(n, BLOCK)] = value
        upper, lower = halves_of(value)
        t_hi[:, pl.ds(n, BLOCK)] = upper
        t_lo[:, pl.ds(n, BLOCK)] = lower
        return carry

    layer((b_hi, b_lo), (out_hi, out_lo), channels, True, keep_outputs)
    live = lax.broadcasted_iota(jnp.int32, (rows, BLOCK), 0) < counts[0]

    def keep_weighted(n, value, carry):
        upper, lower = halves_of(value)
        z_hi[:, pl.ds(n, BLOCK)] = upper
        z_lo[:, pl.ds(n, BLOCK)] = lower
        if with_sums:
            carry = carry + folded(jnp.where(live, value * t_full[:, pl.ds(n, BLOCK)], 0.0))
        return carry

    total = jnp.zeros((8, BLOCK), f32)
    total = layer((t_hi, t_lo), (cov_hi, cov_lo), channels, False, keep_weighted, total)
    if with_sums:
        lane = lax.broadcasted_iota(jnp.int32, (8, 128), 1)
        sums[...] = jnp.where(lane == 3, jnp.sum(total), sums_in[...])


def backward_kernel(
    scale, z_hi, z_lo, gate_one, gate_two, in_hi, in_lo, mid_hi, mid_lo, out_hi, out_lo,
    own_grad, other_grad, a_hi, a_lo, b_hi, b_lo
):
    hidden = mid_hi.shape[0]
    layer((z_hi, z_lo), (out_hi, out_lo), hidden, False, gated(gate_two, (a_hi, a_lo)))
    layer((a_hi, a_lo), (mid_hi, mid_lo), hidden, True, gated(gate_one, (b_hi, b_lo)))
    for start in range(0, 2 * WIDE, BLOCK):
        value = tile((b_hi, b_lo), (in_hi, in_lo), start, True)
        for first, target in ((0, own_grad), (WIDE, other_grad)):
            low, top = max(start, first), min(start + BLOCK, first + WIDE)
            if low < top:
                target[:, low - first : top - first] = value[:, low - start : top - start] * scale


def forward_call(counts, own, other, gates, weights, sums):
    rows = own.shape[0]
    hidden, channels = weights[2].shape[0], weights[6].shape[0]
    with_sums = sums is not None
    out = [shape((rows, channels), bf16)] * 2 + [shape((8, 128))] * with_sums
    pair = lambda n: [pltpu.VMEM((rows, n), bf16)] * 2
    args = (counts, own, other, *gates, *weights) + ((sums,) if with_sums else ())
    return call(
        functools.partial(forward_kernel, with_sums),
        out,
        [smem] + [vmem] * (len(args) - 1),
        [vmem] * len(out),
        pair(2 * WIDE)
        + pair(hidden)
        + pair(hidden)
        + [pltpu.VMEM((rows, channels), f32)]
        + pair(channels),
        16,
        13,
    )(*args)


def backward_call(scale, z, gates, weights):
    rows = z[0].shape[0]
    hidden = weights[2].shape[0]
    args = (*z, *gates, *weights[:6])
    return call(
        functools.partial(backward_kernel, scale),
        [shape((rows, WIDE))] * 2,
        [vmem] * len(args),
        [vmem] * 2,
        [pltpu.VMEM((rows, hidden), bf16)] * 4,
        10,
        11,
    )(*args)


def spread_kernel(counts, cells, own, other, coupling, edge, field, south, north, west, east, parts):
    lats, lons, width = field.shape
    slots = own.shape[0]
    chunk = 512
    for k, part in enumerate((own, other)):
        row = lax.broadcasted_iota(jnp.int32, (slots, WIDE), 0)
        upper, lower = halves_of(jnp.where(row < counts[k], part[...], 0.0))
        parts[k, :, 0:WIDE] = upper
        parts[k, :, WIDE : 2 * WIDE] = lower

    def body(b, carry):
        first = b * chunk
        cell = lax.broadcasted_iota(jnp.int32, (chunk, BLOCK), 0) + first
        lat = pl.ds(b * (chunk // lons), chunk // lons)

        def piece(k, s):
            hot = (cell == cells[k : k + 1, s : s + BLOCK]).astype(f32).astype(bf16)
            both = jnp.dot(hot, parts[k, s : s + BLOCK, :], preferred_element_type=f32)
            total = both[:, :WIDE] + both[:, WIDE:]
            return total[:, :width].reshape(chunk // lons, lons, width)

        field[lat] = piece(0, 0) + piece(1, 0)
        for k in range(2):
            for s in range(BLOCK, slots, BLOCK):

                @pl.when(counts[k] > s)
                def _(k=k, s=s):
                    field[lat] += piece(k, s)

        return carry

    lax.fori_loop(0, lats * lons // chunk, body, 0)

    def move(b, carry):
        for k in range(8):
            i = b * 8 + k
            value = field[i]
            west[pl.ds(i, 1), :] = value[:1]
            east[pl.ds(i, 1), :] = value[lons - 1 :]
        return carry

    lax.fori_loop(0, lats // 8, move, 0)
    east[...] = east[...] * edge[:, 0:1]
    west[...] = west[...] * edge[:, 1:2]
    south[0] = field[0] * coupling[0][:, 3:4]
    north[0] = field[lats - 1] * coupling[lats - 1][:, 2:3]


def edge_shapes(lats, lons, width):
    return [shape((1, lons, width))] * 2 + [shape((lats, width))] * 2


def spread_call(counts, cells, own, other, coupling, edge, width):
    lats, lons, _ = coupling.shape
    slots = own.shape[0]
    out = [shape((lats, lons, width))] + edge_shapes(lats, lons, width)
    return call(
        spread_kernel,
        out,
        [smem] + [vmem] * 5,
        [vmem] * 5,
        [pltpu.VMEM((2, slots, 2 * WIDE), bf16)],
        10,
        5,
    )(counts, cells, own, other, coupling, edge)


def adjoint_rows(field, south, north, west, east, coupling, rates, finish, carry, after=None):
    lats, lons, width = field.shape
    rate = rates[...]
    lon = lax.broadcasted_iota(jnp.int32, (lons, width), 0)

    def row(i, below, above, carry):
        value = field[i]
        c = coupling[i]
        flux = below + above
        flux = flux + from_west(c[:, 0:1] * value, west[pl.ds(i, 1), :], lon)
        flux = flux + from_east(c[:, 1:2] * value, east[pl.ds(i, 1), :], lon)
        total = c[:, 0:1] + c[:, 1:2] + c[:, 2:3] + c[:, 3:4]
        return finish(i, value + rate * (flux - total * value), carry)

    def below(i):
        return coupling[i - 1][:, 2:3] * field[i - 1]

    def above(i):
        return coupling[i + 1][:, 3:4] * field[i + 1]

    return sweep(lats, row, below, above, south[0], north[0], carry, after)


def basis_kernel(
    field, south, north, west, east, coupling, rates, right_side, sums_in,
    basis, out_south, out_north, out_west, out_east, sums
):
    lats, lons, width = field.shape

    def finish(i, value, carry):
        basis[i] = value
        out_west[pl.ds(i, 1), :] = value[:1]
        out_east[pl.ds(i, 1), :] = value[lons - 1 :]
        return carry[0] + folded(right_side[i] * value), carry[1] + folded(value * value)

    zero = jnp.zeros((8, width), f32)
    cross, square = adjoint_rows(
        field, south, north, west, east, coupling, rates, finish, (zero, zero)
    )
    out_south[0] = basis[0]
    out_north[0] = basis[lats - 1]
    lane = lax.broadcasted_iota(jnp.int32, (8, 128), 1)
    result = jnp.where(lane == 1, jnp.sum(cross), sums_in[...])
    sums[...] = jnp.where(lane == 2, jnp.sum(square), result)


def basis_call(field, halo, coupling, rates, right_side, sums):
    lats, lons, width = field.shape
    out = [shape((lats, lons, width))] + edge_shapes(lats, lons, width) + [shape((8, 128))]
    return call(basis_kernel, out, [vmem] * 9, [vmem] * 6, [], 6, 4)(
        field, *halo, coupling, rates, right_side, sums
    )


def final_kernel(
    field, south, north, west, east, coupling, rates, right_side, basis, sums,
    solution_out, residual_out, solution_part, residual_part, sems
):
    lats, lons, width = field.shape
    s = sums[0:1, :]
    rr, rv, vv, vy = s[:, 0:1], s[:, 1:2], s[:, 2:3], s[:, 3:4]
    q = SCALE * rv
    den = rr + q
    first_step = rr / den
    p = SCALE * first_step
    rest = q / den
    new = p * p * vv - rest * rest * rr
    a = rest + new / rr
    square = a * a * rr - 2.0 * a * p * rv + p * p * vv
    curve = a * a * q - 2.0 * a * p * (SCALE * vv) + p * p * vy
    step = new / (square + curve)
    k_right = first_step + step * a
    k_basis = -(step * p)
    l_right = rest - step * a
    l_basis = step * p - p - step * a * SCALE
    l_image = step * p
    outs = ((solution_part, solution_out), (residual_part, residual_out))

    def finish(i, value, carry):
        solution_part[i] = k_right * right_side[i] + k_basis * basis[i]
        residual_part[i] = l_right * right_side[i] + l_basis * basis[i] + l_image * value
        return carry

    def start(g):
        rows = pl.ds(g * GROUP, GROUP)
        for k, (part, out) in enumerate(outs):
            pltpu.make_async_copy(part.at[rows], out.at[rows], sems.at[k]).start()

    def after(g):
        if not isinstance(g, int) or g > 0:
            start(g - 1)

    adjoint_rows(field, south, north, west, east, coupling, rates, finish, 0, after)
    start(lats // GROUP - 1)
    for k, (part, out) in enumerate(outs):
        pltpu.make_async_copy(part, out, sems.at[k]).wait()


def final_call(field, halo, coupling, rates, right_side, basis, sums):
    return call(
        final_kernel,
        [shape(field.shape)] * 2,
        [vmem] * 10,
        [hbm] * 2,
        [pltpu.VMEM(field.shape, f32)] * 2 + [pltpu.SemaphoreType.DMA((2,))],
        12,
        6,
    )(field, *halo, coupling, rates, right_side, basis, sums)


def shifted(value, axis, step):
    count = lax.axis_size(axis)
    return lax.ppermute(value, axis, [(i, (i + step) % count) for i in range(count)])


def exchanged(south_row, north_row, west_col, east_col):
    from_west = shifted(east_col, "col", 1)
    from_east = shifted(west_col, "col", -1)
    from_south = shifted(north_row, "row", 1)
    from_north = shifted(south_row, "row", -1)
    return from_south, from_north, from_west, from_east


def swapped(value):
    return lax.ppermute(value, "side", [(0, 1), (1, 0)])


def everyone(values):
    n = 4
    total = values + swapped(values)
    total = total + sum(shifted(total, "row", k) for k in range(1, n))
    size = lax.axis_size("col")
    for low in (True, False):
        base = total
        for k in range(1, n):
            if low:
                pairs = [(c, (c // n) * n + (c % n + k) % n) for c in range(size)]
            else:
                pairs = [(c, ((c // n + k) % n) * n + c % n) for c in range(size)]
            total = total + lax.ppermute(base, "col", pairs)
    return total


def local(
    right_side,
    couplings,
    channel_rates,
    weight_in,
    weight_mid,
    weight_out,
    inverse_cov,
    profile_cells,
    profile_counts,
    gate_first,
    gate_second,
):
    side_index = lax.axis_index("side")
    tile_count = lax.axis_size("row") * lax.axis_size("col")
    tile_index = lax.axis_index("row") * lax.axis_size("col") + lax.axis_index("col")
    lats, lons, width = right_side.shape
    halo = exchanged(
        right_side[:1], right_side[lats - 1 :], right_side[:, 0], right_side[:, lons - 1]
    )
    latitude = lax.axis_index("row") * lats + jnp.arange(lats)
    north_open = (latitude < lats * lax.axis_size("row") - 1)[:, None]
    south_open = (latitude > 0)[:, None]
    planes = [
        couplings[0],
        couplings[1],
        jnp.where(north_open, couplings[2], 0.0),
        jnp.where(south_open, couplings[3], 0.0),
    ]
    coupling = jnp.stack(planes, axis=2)
    edge = jnp.stack([couplings[0, :, lons - 1], couplings[1, :, 0]], axis=1)
    rates = channel_rates[None, :]
    order = jnp.stack([side_index, 1 - side_index])
    cells = jnp.clip(profile_cells[order], 0, lats * lons - 1)
    counts = profile_counts[order * tile_count + tile_index]
    weights = prepare_call(
        order[:1], weight_in, weight_mid, weight_out.T, inverse_cov, 3 * BLOCK
    )
    gates = (gate_first, gate_second)

    own, other, sums = tangent_call(True, cells, counts, right_side, halo, coupling, rates)
    z = forward_call(counts, own, swapped(other), gates, weights, None)
    own, other = backward_call(1.0 / SCALE, z, gates, weights)
    field, *out = spread_call(counts, cells, own, swapped(other), coupling, edge, width)
    halo = exchanged(*out)
    basis, *out, sums = basis_call(field, halo, coupling, rates, right_side, sums)
    halo = exchanged(*out)
    own, other = tangent_call(False, cells, counts, basis, halo, coupling, rates)
    *z, sums = forward_call(counts, own, swapped(other), gates, weights, sums)
    sums = everyone(sums)
    own, other = backward_call(1.0, z, gates, weights)
    field, *out = spread_call(counts, cells, own, swapped(other), coupling, edge, width)
    halo = exchanged(*out)
    return tuple(final_call(field, halo, coupling, rates, right_side, basis, sums))


def solution(mesh):
    in_specs = (
        P("row", "col", "side"),
        P(None, "row", "col"),
        P("side"),
        P(),
        P(),
        P(),
        P(),
        P(None, ("row", "col")),
        P(),
        P(("side", "row", "col"), None),
        P(("side", "row", "col"), None),
    )
    out_specs = (P("row", "col", "side"), P("row", "col", "side"))
    return jax.shard_map(local, mesh=mesh, in_specs=in_specs, out_specs=out_specs, check_vma=False)
```

```python
import functools

import jax
import jax.numpy as jnp
from jax import lax
from jax.experimental import pallas as pl
from jax.experimental.pallas import tpu as pltpu
from jax.sharding import PartitionSpec as P

SCALE = 2.0**40
BLOCK = 256
f32, bf16 = jnp.float32, jnp.bfloat16
vmem = pl.BlockSpec(memory_space=pltpu.VMEM)
smem = pl.BlockSpec(memory_space=pltpu.SMEM)
hbm = pl.BlockSpec(memory_space=pl.ANY)


WIDE = 384
GROUP = 4


def shape(dims, dtype=f32):
    return jax.ShapeDtypeStruct(dims, dtype)


def call(kernel, out, in_specs, out_specs, scratch, mib, micros):
    return pl.pallas_call(
        kernel,
        out_shape=out,
        in_specs=in_specs,
        out_specs=out_specs,
        scratch_shapes=scratch,
        compiler_params=pltpu.CompilerParams(vmem_limit_bytes=mib << 20),
        cost_estimate=pl.CostEstimate(
            flops=int(micros * 1e9), bytes_accessed=int(micros * 3e6), transcendentals=0
        ),
    )


def halves_of(value):
    upper = value.astype(bf16)
    return upper, (value - upper.astype(f32)).astype(bf16)


def folded(value):
    rows, width = value.shape
    return jnp.sum(value.reshape(rows // 8, 8, width), axis=0)


def lane_vector(scalars):
    lane = lax.broadcasted_iota(jnp.int32, (8, 128), 1)
    result = jnp.zeros((8, 128), f32)
    for k, value in enumerate(scalars):
        result = jnp.where(lane == k, value, result)
    return result


def from_west(value, west_row, lon):
    last = value.shape[0] - 1
    return jnp.where(lon == 0, west_row, jnp.concatenate([value[last:], value[:last]], axis=0))


def from_east(value, east_row, lon):
    last = value.shape[0] - 1
    return jnp.where(lon == last, east_row, jnp.concatenate([value[1:], value[:1]], axis=0))


def sweep(lats, row, below, above, south, north, carry, after=None):
    def group(g, low, high, carry):
        for k in range(GROUP):
            i = g * GROUP + k
            under = south if low and k == 0 else below(i)
            over = north if high and k == GROUP - 1 else above(i)
            carry = row(i, under, over, carry)
        if after is not None:
            after(g)
        return carry

    last = lats // GROUP - 1
    carry = group(0, True, False, carry)
    carry = lax.fori_loop(1, last, lambda g, c: group(g, False, False, c), carry)
    return group(last, False, True, carry)


def prepare_kernel(
    side, w_in, w_mid, w_out, cov, in_hi, in_lo, mid_hi, mid_lo, out_hi, out_lo, cov_hi, cov_lo,
    s_in, s_cov, s_out, s_mid, sems
):
    sources = ((w_in, s_in), (cov, s_cov), (w_out, s_out), (w_mid, s_mid))
    copies = [pltpu.make_async_copy(a, b, sems.at[k]) for k, (a, b) in enumerate(sources)]
    for copy in copies:
        copy.start()
    for target in (in_hi, in_lo, out_hi, out_lo, cov_hi, cov_lo):
        target[...] = jnp.zeros_like(target)
    half = w_in.shape[0] // 2
    hidden = w_mid.shape[0]
    channels = cov.shape[0]

    def columns(total, step, move):
        def body(k, carry):
            move(pl.ds(pl.multiple_of(k * step, step), step))
            return carry

        lax.fori_loop(0, total // step, body, 0)
        if total % step:
            move(slice(total - total % step, total))

    copies[0].wait()
    for flag in range(2):

        @pl.when(side[0] == flag)
        def _(flag=flag):
            for target, source in ((0, flag * half), (WIDE, (1 - flag) * half)):

                def move(n, target=target, source=source):
                    upper, lower = halves_of(s_in[source : source + half, n])
                    in_hi[target : target + half, n] = upper
                    in_lo[target : target + half, n] = lower

                columns(hidden, 128, move)

    copies[1].wait()

    def move_cov(n):
        upper, lower = halves_of(s_cov[:, n])
        cov_hi[:channels, n] = upper
        cov_lo[:channels, n] = lower

    columns(channels, 128, move_cov)
    copies[2].wait()

    def move_out(n):
        upper, lower = halves_of(s_out[:, n])
        out_hi[:channels, n] = upper
        out_lo[:channels, n] = lower

    columns(hidden, 128, move_out)
    copies[3].wait()

    def move_mid(n):
        upper, lower = halves_of(s_mid[n, :])
        mid_hi[n, :] = upper
        mid_lo[n, :] = lower

    columns(hidden, 64, move_mid)


def prepare_call(side, w_in, w_mid, w_out, cov, channels):
    hidden = w_mid.shape[0]
    dims = [(2 * WIDE, hidden), (hidden, hidden), (channels, hidden), (channels, channels)]
    out = [shape(d, bf16) for d in dims for _ in range(2)]
    return call(
        prepare_kernel,
        out,
        [smem] + [hbm] * 4,
        [vmem] * 8,
        [pltpu.VMEM(m.shape, f32) for m in (w_in, cov, w_out, w_mid)]
        + [pltpu.SemaphoreType.DMA((4,))],
        16,
        5,
    )(side, w_in, w_mid, w_out, cov)


def tangent_kernel(
    with_square, cells, counts, field, south, north, west, east, coupling, rates, own, other, *rest
):
    image = rest[-1]
    lats, lons, width = field.shape
    rate = rates[...]
    tail = width - 256
    lon = lax.broadcasted_iota(jnp.int32, (lons, width), 0)
    image[2] = jnp.zeros_like(image[2])

    def row(i, below, above, total):
        value = field[i]
        c = coupling[i]
        to_west = from_west(value, west[pl.ds(i, 1), :], lon)
        to_east = from_east(value, east[pl.ds(i, 1), :], lon)
        flux = c[:, 0:1] * (to_east - value)
        flux = flux + c[:, 1:2] * (to_west - value)
        flux = flux + c[:, 2:3] * (above - value)
        flux = flux + c[:, 3:4] * (below - value)
        result = value + rate * flux
        rows = pl.ds(i * lons if isinstance(i, int) else pl.multiple_of(i * lons, lons), lons)
        image[0, rows, :] = result[:, 0:128]
        image[1, rows, :] = result[:, 128:256]
        image[2, rows, 0:tail] = result[:, 256:]
        if with_square:
            total = total + folded(value * value)
        return total

    total = jnp.zeros((8, width), f32)
    total = sweep(
        lats, row, lambda i: field[i - 1], lambda i: field[i + 1], south[0], north[0], total
    )
    if with_square:
        rest[0][...] = lane_vector([jnp.sum(total)])

    def gather(which, out):
        def body(b, carry):
            first = pl.multiple_of(b * 8, 8)
            found = [cells[which, first + k] for k in range(8)]
            rows = [[image[t, pl.ds(cell, 1), :] for t in range(3)] for cell in found]
            for k in range(8):
                out[pl.ds(first + k, 1), :] = jnp.concatenate(rows[k], axis=1)
            return carry

        lax.fori_loop(0, (counts[which] + 7) // 8, body, 0)

    gather(1, other)
    gather(0, own)


def tangent_call(with_square, cells, counts, field, halo, coupling, rates):
    lats, lons, _ = field.shape
    slots = cells.shape[1]
    out = [shape((slots, WIDE))] * 2 + [shape((8, 128))] * with_square
    return call(
        functools.partial(tangent_kernel, with_square),
        out,
        [smem, smem] + [vmem] * 7,
        [vmem] * len(out),
        [pltpu.VMEM((3, lats * lons, 128), f32)],
        8,
        6,
    )(cells, counts, field, *halo, coupling, rates)


def tile(left, right, n, transposed):
    hi, lo = left
    if transposed:
        pick = [w[pl.ds(n, BLOCK), :] for w in right]
        dims = (((1,), (1,)), ((), ()))
    else:
        pick = [w[:, pl.ds(n, BLOCK)] for w in right]
        dims = (((1,), (0,)), ((), ()))
    dot = functools.partial(lax.dot_general, dimension_numbers=dims, preferred_element_type=f32)
    upper = hi[...]
    return dot(upper, pick[0]) + dot(upper, pick[1]) + dot(lo[...], pick[0])


def layer(left, right, columns, transposed, finish, held, carry=0):
    steps = columns // BLOCK

    def body(k, carry):
        value = tile(left, right, pl.multiple_of(k * BLOCK, BLOCK), transposed)
        n = pl.multiple_of(jnp.maximum(k - 1, 0) * BLOCK, BLOCK)
        after = finish(n, held[...], carry)
        held[...] = value
        return jax.tree.map(lambda new, old: jnp.where(k > 0, new, old), after, carry)

    carry = lax.fori_loop(0, steps, body, carry)
    return finish((steps - 1) * BLOCK, held[...], carry)


def gated(gate, target):
    def finish(n, value, carry):
        upper, lower = halves_of(value * gate[:, pl.ds(n, BLOCK)].astype(f32))
        target[0][:, pl.ds(n, BLOCK)] = upper
        target[1][:, pl.ds(n, BLOCK)] = lower
        return carry

    return finish


def forward_kernel(
    with_sums, counts, own, other, gate_one, gate_two,
    in_hi, in_lo, mid_hi, mid_lo, out_hi, out_lo, cov_hi, cov_lo, *rest
):
    if with_sums:
        sums_in, z_hi, z_lo, sums = rest[:4]
    else:
        z_hi, z_lo = rest[:2]
    x_hi, x_lo, a_hi, a_lo, b_hi, b_lo, t_full, t_hi, t_lo, held = rest[-10:]
    rows = own.shape[0]
    for start, part in ((0, own), (WIDE, other)):
        upper, lower = halves_of(part[...])
        x_hi[:, start : start + WIDE] = upper
        x_lo[:, start : start + WIDE] = lower
    hidden = mid_hi.shape[0]
    channels = cov_hi.shape[0]
    layer((x_hi, x_lo), (in_hi, in_lo), hidden, False, gated(gate_one, (a_hi, a_lo)), held)
    layer((a_hi, a_lo), (mid_hi, mid_lo), hidden, False, gated(gate_two, (b_hi, b_lo)), held)

    def keep_outputs(n, value, carry):
        if with_sums:
            t_full[:, pl.ds(n, BLOCK)] = value
        upper, lower = halves_of(value)
        t_hi[:, pl.ds(n, BLOCK)] = upper
        t_lo[:, pl.ds(n, BLOCK)] = lower
        return carry

    layer((b_hi, b_lo), (out_hi, out_lo), channels, True, keep_outputs, held)
    live = lax.broadcasted_iota(jnp.int32, (rows, BLOCK), 0) < counts[0]

    def keep_weighted(n, value, carry):
        upper, lower = halves_of(value)
        z_hi[:, pl.ds(n, BLOCK)] = upper
        z_lo[:, pl.ds(n, BLOCK)] = lower
        if with_sums:
            carry = carry + folded(jnp.where(live, value * t_full[:, pl.ds(n, BLOCK)], 0.0))
        return carry

    total = jnp.zeros((8, BLOCK), f32)
    total = layer((t_hi, t_lo), (cov_hi, cov_lo), channels, False, keep_weighted, held, total)
    if with_sums:
        lane = lax.broadcasted_iota(jnp.int32, (8, 128), 1)
        sums[...] = jnp.where(lane == 3, jnp.sum(total), sums_in[...])


def backward_kernel(
    z_hi, z_lo, gate_one, gate_two, mid_hi, mid_lo, out_hi, out_lo, b_hi, b_lo, a_hi, a_lo, held
):
    hidden = mid_hi.shape[0]
    layer((z_hi, z_lo), (out_hi, out_lo), hidden, False, gated(gate_two, (a_hi, a_lo)), held)
    layer((a_hi, a_lo), (mid_hi, mid_lo), hidden, True, gated(gate_one, (b_hi, b_lo)), held)


def gradient_kernel(scale, b_hi, b_lo, in_hi, in_lo, own_grad, other_grad):
    for start in range(0, 2 * WIDE, BLOCK):
        value = tile((b_hi, b_lo), (in_hi, in_lo), start, True)
        for first, target in ((0, own_grad), (WIDE, other_grad)):
            low, top = max(start, first), min(start + BLOCK, first + WIDE)
            if low < top:
                target[:, low - first : top - first] = value[:, low - start : top - start] * scale


def forward_call(counts, own, other, gates, weights, sums):
    rows = own.shape[0]
    hidden, channels = weights[2].shape[0], weights[6].shape[0]
    with_sums = sums is not None
    out = [shape((rows, channels), bf16)] * 2 + [shape((8, 128))] * with_sums
    pair = lambda n: [pltpu.VMEM((rows, n), bf16)] * 2
    args = (counts, own, other, *gates, *weights) + ((sums,) if with_sums else ())
    return call(
        functools.partial(forward_kernel, with_sums),
        out,
        [smem] + [vmem] * (len(args) - 1),
        [vmem] * len(out),
        pair(2 * WIDE)
        + pair(hidden)
        + pair(hidden)
        + [pltpu.VMEM((rows, channels), f32)]
        + pair(channels)
        + [pltpu.VMEM((rows, BLOCK), f32)],
        16,
        13,
    )(*args)


def backward_call(z, gates, weights):
    rows = z[0].shape[0]
    hidden = weights[2].shape[0]
    args = (*z, *gates, *weights[2:6])
    return call(
        backward_kernel,
        [shape((rows, hidden), bf16)] * 2,
        [vmem] * len(args),
        [vmem] * 2,
        [pltpu.VMEM((rows, hidden), bf16)] * 2 + [pltpu.VMEM((rows, BLOCK), f32)],
        10,
        8,
    )(*args)


def gradient_call(scale, back, weights):
    rows = back[0].shape[0]
    return call(
        functools.partial(gradient_kernel, scale),
        [shape((rows, WIDE))] * 2,
        [vmem] * 4,
        [vmem] * 2,
        [],
        8,
        3,
    )(*back, *weights[:2])


def hot_rows(cell, cells):
    return (cell == cells).astype(f32).astype(bf16)


def merged(both):
    return both[:, :WIDE] + both[:, WIDE:]


def edge_kernel(
    counts, cells, own, other, coupling, columns, parts, south, north, west, east, *lines
):
    lats, lons, _ = coupling.shape
    slots = own.shape[0]
    width = west.shape[1]
    for k, part in enumerate((own, other)):
        row = lax.broadcasted_iota(jnp.int32, (slots, WIDE), 0)
        upper, lower = halves_of(jnp.where(row < counts[k], part[...], 0.0))
        parts[k, :, 0:WIDE] = upper
        parts[k, :, WIDE : 2 * WIDE] = lower
    total = 4 * lats + 4 * lons
    r = lax.broadcasted_iota(jnp.int32, (total, BLOCK), 0)
    cell = jnp.full_like(r, -1)
    start = 0
    spans = []
    for lon in (0, 1, lons - 2, lons - 1):
        inside = (r >= start) & (r < start + lats)
        cell = jnp.where(inside, (r - start) * lons + lon, cell)
        spans.append((start, lats))
        start += lats
    for lat in (0, 1, lats - 2, lats - 1):
        inside = (r >= start) & (r < start + lons)
        cell = jnp.where(inside, r - start + lat * lons, cell)
        spans.append((start, lons))
        start += lons
    value = jnp.zeros((total, 2 * WIDE), f32)
    for k in range(2):
        for s in range(0, slots, BLOCK):
            hot = hot_rows(cell, cells[k : k + 1, s : s + BLOCK])
            value = value + jnp.dot(hot, parts[k, s : s + BLOCK, :], preferred_element_type=f32)
    value = merged(value)[:, :width]
    for line, (start, count) in zip(lines, spans):
        line[...] = value[start : start + count]
    west[...] = lines[0][...] * columns[:, 1:2]
    east[...] = lines[3][...] * columns[:, 0:1]
    south[0] = lines[4][...] * coupling[0][:, 3:4]
    north[0] = lines[7][...] * coupling[lats - 1][:, 2:3]


def edge_shapes(lats, lons, width):
    return [shape((1, lons, width))] * 2 + [shape((lats, width))] * 2


def edge_call(counts, cells, own, other, coupling, columns, width):
    lats, lons, _ = coupling.shape
    slots = own.shape[0]
    out = [shape((2, slots, 2 * WIDE), bf16)] + edge_shapes(lats, lons, width)
    out += [shape((lats, width))] * 4 + [shape((lons, width))] * 4
    return call(edge_kernel, out, [smem] + [vmem] * 5, [vmem] * len(out), [], 12, 2)(
        counts, cells, own, other, coupling, columns
    )


def spread_kernel(counts, cells, parts, field):
    lats, lons, width = field.shape
    slots = parts.shape[1]
    chunk = 512

    def body(b, carry):
        first = b * chunk
        cell = lax.broadcasted_iota(jnp.int32, (chunk, BLOCK), 0) + first
        lat = pl.ds(b * (chunk // lons), chunk // lons)

        def piece(k, s):
            hot = hot_rows(cell, cells[k : k + 1, s : s + BLOCK])
            both = jnp.dot(hot, parts[k, s : s + BLOCK, :], preferred_element_type=f32)
            return merged(both)[:, :width].reshape(chunk // lons, lons, width)

        field[lat] = piece(0, 0) + piece(1, 0)
        for k in range(2):
            for s in range(BLOCK, slots, BLOCK):

                @pl.when(counts[k] > s)
                def _(k=k, s=s):
                    field[lat] += piece(k, s)

        return carry

    lax.fori_loop(0, lats * lons // chunk, body, 0)


def spread_call(counts, cells, parts, lats, lons, width):
    return call(
        spread_kernel,
        [shape((lats, lons, width))],
        [smem] + [vmem] * 2,
        [vmem],
        [],
        8,
        4,
    )(counts, cells, parts)[0]


def border_kernel(
    south, north, west, east, w0, w1, e1, e0, s0, s1, n1, n0, coupling, columns, rates,
    out_south, out_north, out_west, out_east
):
    lats, width = w0.shape
    lons = s0.shape[0]
    rate = rates[...]
    lat = lax.broadcasted_iota(jnp.int32, (lats, width), 0)
    lon = lax.broadcasted_iota(jnp.int32, (lons, width), 0)

    def column(line, inner, halo, first, target, end):
        c = [columns[:, first + k : first + k + 1] for k in range(4)]
        value = line[...]
        flux = halo[...] + c[0] * inner[...]
        flux = flux + from_west(c[1] * value, south[0, end : end + 1, :], lat)
        flux = flux + from_east(c[2] * value, north[0, end : end + 1, :], lat)
        target[...] = value + rate * (flux - c[3] * value)

    column(w0, w1, west, 2, out_west, 0)
    column(e0, e1, east, 6, out_east, lons - 1)

    def along(i, line, flux):
        c = coupling[i]
        value = line[...]
        flux = flux + from_west(c[:, 0:1] * value, west[i : i + 1, :], lon)
        flux = flux + from_east(c[:, 1:2] * value, east[i : i + 1, :], lon)
        return value + rate * (flux - c[:, 4:5] * value)

    out_south[0] = along(0, s0, south[0] + coupling[1][:, 3:4] * s1[...])
    out_north[0] = along(lats - 1, n0, north[0] + coupling[lats - 2][:, 2:3] * n1[...])


def border_call(halo, lines, coupling, columns, rates):
    lats, width = lines[0].shape
    out = edge_shapes(lats, lines[4].shape[0], width)
    return call(border_kernel, out, [vmem] * 15, [vmem] * 4, [], 4, 1)(
        *halo, *lines, coupling, columns, rates
    )


def adjoint_rows(field, south, north, west, east, coupling, rates, finish, carry, after=None):
    lats, lons, width = field.shape
    rate = rates[...]
    lon = lax.broadcasted_iota(jnp.int32, (lons, width), 0)

    def row(i, below, above, carry):
        value = field[i]
        c = coupling[i]
        flux = below + above
        flux = flux + from_west(c[:, 0:1] * value, west[pl.ds(i, 1), :], lon)
        flux = flux + from_east(c[:, 1:2] * value, east[pl.ds(i, 1), :], lon)
        return finish(i, value + rate * (flux - c[:, 4:5] * value), carry)

    def below(i):
        return coupling[i - 1][:, 2:3] * field[i - 1]

    def above(i):
        return coupling[i + 1][:, 3:4] * field[i + 1]

    return sweep(lats, row, below, above, south[0], north[0], carry, after)


def basis_kernel(
    field, south, north, west, east, coupling, rates, right_side, sums_in, basis, sums
):
    _, _, width = field.shape

    def finish(i, value, carry):
        basis[i] = value
        return carry[0] + folded(right_side[i] * value), carry[1] + folded(value * value)

    zero = jnp.zeros((8, width), f32)
    cross, square = adjoint_rows(
        field, south, north, west, east, coupling, rates, finish, (zero, zero)
    )
    lane = lax.broadcasted_iota(jnp.int32, (8, 128), 1)
    result = jnp.where(lane == 1, jnp.sum(cross), sums_in[...])
    sums[...] = jnp.where(lane == 2, jnp.sum(square), result)


def basis_call(field, halo, coupling, rates, right_side, sums):
    out = [shape(field.shape), shape((8, 128))]
    return call(basis_kernel, out, [vmem] * 9, [vmem] * 2, [], 6, 5)(
        field, *halo, coupling, rates, right_side, sums
    )


def final_kernel(
    field, south, north, west, east, coupling, rates, right_side, basis, sums,
    solution_out, residual_out, solution_part, residual_part, sems
):
    lats, _, _ = field.shape
    s = sums[0:1, :]
    rr, rv, vv, vy = s[:, 0:1], s[:, 1:2], s[:, 2:3], s[:, 3:4]
    q = SCALE * rv
    den = rr + q
    first_step = rr / den
    p = SCALE * first_step
    rest = q / den
    new = p * p * vv - rest * rest * rr
    a = rest + new / rr
    square = a * a * rr - 2.0 * a * p * rv + p * p * vv
    curve = a * a * q - 2.0 * a * p * (SCALE * vv) + p * p * vy
    step = new / (square + curve)
    k_right = first_step + step * a
    k_basis = -(step * p)
    l_right = rest - step * a
    l_basis = step * p - p - step * a * SCALE
    l_image = step * p
    outs = ((solution_part, solution_out), (residual_part, residual_out))

    def finish(i, value, carry):
        solution_part[i] = k_right * right_side[i] + k_basis * basis[i]
        residual_part[i] = l_right * right_side[i] + l_basis * basis[i] + l_image * value
        return carry

    def start(g):
        rows = pl.ds(g * GROUP, GROUP)
        for k, (part, out) in enumerate(outs):
            pltpu.make_async_copy(part.at[rows], out.at[rows], sems.at[k]).start()

    def after(g):
        if not isinstance(g, int) or g > 0:
            start(g - 1)

    adjoint_rows(field, south, north, west, east, coupling, rates, finish, 0, after)
    start(lats // GROUP - 1)
    for k, (part, out) in enumerate(outs):
        pltpu.make_async_copy(part, out, sems.at[k]).wait()


def final_call(field, halo, coupling, rates, right_side, basis, sums):
    return call(
        final_kernel,
        [shape(field.shape)] * 2,
        [vmem] * 10,
        [hbm] * 2,
        [pltpu.VMEM(field.shape, f32)] * 2 + [pltpu.SemaphoreType.DMA((2,))],
        12,
        6,
    )(field, *halo, coupling, rates, right_side, basis, sums)


def shifted(value, axis, step):
    count = lax.axis_size(axis)
    return lax.ppermute(value, axis, [(i, (i + step) % count) for i in range(count)])


def exchanged(south_row, north_row, west_col, east_col):
    from_west = shifted(east_col, "col", 1)
    from_east = shifted(west_col, "col", -1)
    from_south = shifted(north_row, "row", 1)
    from_north = shifted(south_row, "row", -1)
    return from_south, from_north, from_west, from_east


def swapped(value):
    return lax.ppermute(value, "side", [(0, 1), (1, 0)])


def everyone(values):
    n = 4
    total = values + swapped(values)
    total = total + sum(shifted(total, "row", k) for k in range(1, n))
    size = lax.axis_size("col")
    for low in (True, False):
        base = total
        for k in range(1, n):
            if low:
                pairs = [(c, (c // n) * n + (c % n + k) % n) for c in range(size)]
            else:
                pairs = [(c, ((c // n + k) % n) * n + c % n) for c in range(size)]
            total = total + lax.ppermute(base, "col", pairs)
    return total


def local(
    right_side,
    couplings,
    channel_rates,
    weight_in,
    weight_mid,
    weight_out,
    inverse_cov,
    profile_cells,
    profile_counts,
    gate_first,
    gate_second,
):
    side_index = lax.axis_index("side")
    tile_count = lax.axis_size("row") * lax.axis_size("col")
    tile_index = lax.axis_index("row") * lax.axis_size("col") + lax.axis_index("col")
    lats, lons, width = right_side.shape
    halo = exchanged(
        right_side[:1], right_side[lats - 1 :], right_side[:, 0], right_side[:, lons - 1]
    )
    latitude = lax.axis_index("row") * lats + jnp.arange(lats)
    north_open = (latitude < lats * lax.axis_size("row") - 1)[:, None]
    south_open = (latitude > 0)[:, None]
    planes = [
        couplings[0],
        couplings[1],
        jnp.where(north_open, couplings[2], 0.0),
        jnp.where(south_open, couplings[3], 0.0),
    ]
    planes.append(planes[0] + planes[1] + planes[2] + planes[3])
    coupling = jnp.stack(planes, axis=2)
    pick = ((0, lons - 1), (1, 0), (1, 1), (2, 0), (3, 0), (4, 0))
    pick += ((0, lons - 2), (2, lons - 1), (3, lons - 1), (4, lons - 1))
    columns = jnp.stack([planes[k][:, j] for k, j in pick], axis=1)
    rates = channel_rates[None, :]
    order = jnp.stack([side_index, 1 - side_index])
    cells = jnp.clip(profile_cells[order], 0, lats * lons - 1)
    counts = profile_counts[order * tile_count + tile_index]
    weights = prepare_call(
        order[:1], weight_in, weight_mid, weight_out.T, inverse_cov, 3 * BLOCK
    )
    gates = (gate_first, gate_second)

    own, other, sums = tangent_call(True, cells, counts, right_side, halo, coupling, rates)
    z = forward_call(counts, own, swapped(other), gates, weights, None)
    back = backward_call(z, gates, weights)
    own, other = gradient_call(1.0 / SCALE, back, weights)
    other = swapped(other)
    parts, *out = edge_call(counts, cells, own, other, coupling, columns, width)
    halo = exchanged(*out[:4])
    field = spread_call(counts, cells, parts, lats, lons, width)
    outer = border_call(halo, out[4:], coupling, columns, rates)
    outer = exchanged(*outer)
    basis, sums = basis_call(field, halo, coupling, rates, right_side, sums)
    own, other = tangent_call(False, cells, counts, basis, outer, coupling, rates)
    *z, sums = forward_call(counts, own, swapped(other), gates, weights, sums)
    sums = everyone(sums)
    back = backward_call(z, gates, weights)
    own, other = gradient_call(1.0, back, weights)
    other = swapped(other)
    parts, *out = edge_call(counts, cells, own, other, coupling, columns, width)
    halo = exchanged(*out[:4])
    field = spread_call(counts, cells, parts, lats, lons, width)
    return tuple(final_call(field, halo, coupling, rates, right_side, basis, sums))


def solution(mesh):
    in_specs = (
        P("row", "col", "side"),
        P(None, "row", "col"),
        P("side"),
        P(),
        P(),
        P(),
        P(),
        P(None, ("row", "col")),
        P(),
        P(("side", "row", "col"), None),
        P(("side", "row", "col"), None),
    )
    out_specs = (P("row", "col", "side"), P("row", "col", "side"))
    return jax.shard_map(local, mesh=mesh, in_specs=in_specs, out_specs=out_specs, check_vma=False)
```

```python
import functools

import jax
import jax.numpy as jnp
from jax import lax
from jax.experimental import pallas as pl
from jax.experimental.pallas import tpu as pltpu
from jax.sharding import PartitionSpec as P

SCALE = 2.0**40
BLOCK = 256
f32, bf16 = jnp.float32, jnp.bfloat16
vmem = pl.BlockSpec(memory_space=pltpu.VMEM)
smem = pl.BlockSpec(memory_space=pltpu.SMEM)
hbm = pl.BlockSpec(memory_space=pl.ANY)


WIDE = 384
GROUP = 4


def shape(dims, dtype=f32):
    return jax.ShapeDtypeStruct(dims, dtype)


def call(kernel, out, in_specs, out_specs, scratch, mib, micros):
    return pl.pallas_call(
        kernel,
        out_shape=out,
        in_specs=in_specs,
        out_specs=out_specs,
        scratch_shapes=scratch,
        compiler_params=pltpu.CompilerParams(vmem_limit_bytes=mib << 20),
        cost_estimate=pl.CostEstimate(
            flops=int(micros * 1e9), bytes_accessed=int(micros * 3e6), transcendentals=0
        ),
    )


def halves_of(value):
    upper = value.astype(bf16)
    return upper, (value - upper.astype(f32)).astype(bf16)


def folded(value):
    rows, width = value.shape
    return jnp.sum(value.reshape(rows // 8, 8, width), axis=0)


def lane_vector(scalars):
    lane = lax.broadcasted_iota(jnp.int32, (8, 128), 1)
    result = jnp.zeros((8, 128), f32)
    for k, value in enumerate(scalars):
        result = jnp.where(lane == k, value, result)
    return result


def from_west(value, west_row, lon):
    last = value.shape[0] - 1
    return jnp.where(lon == 0, west_row, jnp.concatenate([value[last:], value[:last]], axis=0))


def from_east(value, east_row, lon):
    last = value.shape[0] - 1
    return jnp.where(lon == last, east_row, jnp.concatenate([value[1:], value[:1]], axis=0))


def sweep(lats, row, below, above, south, north, carry, after=None):
    def group(g, low, high, carry):
        for k in range(GROUP):
            i = g * GROUP + k
            under = south if low and k == 0 else below(i)
            over = north if high and k == GROUP - 1 else above(i)
            carry = row(i, under, over, carry)
        if after is not None:
            after(g)
        return carry

    last = lats // GROUP - 1
    carry = group(0, True, False, carry)
    carry = lax.fori_loop(1, last, lambda g, c: group(g, False, False, c), carry)
    return group(last, False, True, carry)


def prepare_kernel(
    side, w_in, w_mid, w_out, cov, in_hi, in_lo, mid_hi, mid_lo, out_hi, out_lo, cov_hi, cov_lo,
    s_in, s_cov, s_out, s_mid, sems
):
    sources = ((w_in, s_in), (cov, s_cov), (w_out, s_out), (w_mid, s_mid))
    copies = [pltpu.make_async_copy(a, b, sems.at[k]) for k, (a, b) in enumerate(sources)]
    for copy in copies:
        copy.start()
    for target in (in_hi, in_lo, out_hi, out_lo, cov_hi, cov_lo):
        target[...] = jnp.zeros_like(target)
    half = w_in.shape[0] // 2
    hidden = w_mid.shape[0]
    channels = cov.shape[0]

    def columns(total, step, move):
        def body(k, carry):
            move(pl.ds(pl.multiple_of(k * step, step), step))
            return carry

        lax.fori_loop(0, total // step, body, 0)
        if total % step:
            move(slice(total - total % step, total))

    copies[0].wait()
    for flag in range(2):

        @pl.when(side[0] == flag)
        def _(flag=flag):
            for target, source in ((0, flag * half), (WIDE, (1 - flag) * half)):

                def move(n, target=target, source=source):
                    upper, lower = halves_of(s_in[source : source + half, n])
                    in_hi[target : target + half, n] = upper
                    in_lo[target : target + half, n] = lower

                columns(hidden, 128, move)

    copies[1].wait()

    def move_cov(n):
        upper, lower = halves_of(s_cov[:, n])
        cov_hi[:channels, n] = upper
        cov_lo[:channels, n] = lower

    columns(channels, 128, move_cov)
    copies[2].wait()

    def move_out(n):
        upper, lower = halves_of(s_out[:, n])
        out_hi[:channels, n] = upper
        out_lo[:channels, n] = lower

    columns(hidden, 128, move_out)
    copies[3].wait()

    def move_mid(n):
        upper, lower = halves_of(s_mid[n, :])
        mid_hi[n, :] = upper
        mid_lo[n, :] = lower

    columns(hidden, 64, move_mid)


def prepare_call(side, w_in, w_mid, w_out, cov, channels):
    hidden = w_mid.shape[0]
    dims = [(2 * WIDE, hidden), (hidden, hidden), (channels, hidden), (channels, channels)]
    out = [shape(d, bf16) for d in dims for _ in range(2)]
    return call(
        prepare_kernel,
        out,
        [smem] + [hbm] * 4,
        [vmem] * 8,
        [pltpu.VMEM(m.shape, f32) for m in (w_in, cov, w_out, w_mid)]
        + [pltpu.SemaphoreType.DMA((4,))],
        16,
        5,
    )(side, w_in, w_mid, w_out, cov)


def tangent_kernel(
    with_square, cells, counts, field, south, north, west, east, coupling, rates, own, other, *rest
):
    image = rest[-1]
    lats, lons, width = field.shape
    rate = rates[...]
    tail = width - 256
    lon = lax.broadcasted_iota(jnp.int32, (lons, width), 0)
    image[2] = jnp.zeros_like(image[2])

    def row(i, below, above, total):
        value = field[i]
        c = coupling[i]
        to_west = from_west(value, west[pl.ds(i, 1), :], lon)
        to_east = from_east(value, east[pl.ds(i, 1), :], lon)
        flux = c[:, 0:1] * (to_east - value)
        flux = flux + c[:, 1:2] * (to_west - value)
        flux = flux + c[:, 2:3] * (above - value)
        flux = flux + c[:, 3:4] * (below - value)
        result = value + rate * flux
        rows = pl.ds(i * lons if isinstance(i, int) else pl.multiple_of(i * lons, lons), lons)
        image[0, rows, :] = result[:, 0:128]
        image[1, rows, :] = result[:, 128:256]
        image[2, rows, 0:tail] = result[:, 256:]
        if with_square:
            total = total + folded(value * value)
        return total

    total = jnp.zeros((8, width), f32)
    total = sweep(
        lats, row, lambda i: field[i - 1], lambda i: field[i + 1], south[0], north[0], total
    )
    if with_square:
        rest[0][...] = lane_vector([jnp.sum(total)])

    place = lax.broadcasted_iota(jnp.int32, (8, 128), 0)

    def gather(which, out):
        def body(b, carry):
            first = pl.multiple_of(b * 8, 8)
            found = [cells[which, first + k] for k in range(8)]
            for t in range(3):
                block = image[t, pl.ds(found[0], 8, stride=0), :]
                for k in range(1, 8):
                    block = jnp.where(place == k, image[t, pl.ds(found[k], 8, stride=0), :], block)
                out[pl.ds(first, 8), t * 128 : (t + 1) * 128] = block
            return carry

        lax.fori_loop(0, (counts[which] + 7) // 8, body, 0)

    gather(1, other)
    gather(0, own)


def tangent_call(with_square, cells, counts, field, halo, coupling, rates):
    lats, lons, _ = field.shape
    slots = cells.shape[1]
    out = [shape((slots, WIDE))] * 2 + [shape((8, 128))] * with_square
    return call(
        functools.partial(tangent_kernel, with_square),
        out,
        [smem, smem] + [vmem] * 7,
        [vmem] * len(out),
        [pltpu.VMEM((3, lats * lons, 128), f32)],
        8,
        6,
    )(cells, counts, field, *halo, coupling, rates)


def tile(left, right, n, transposed):
    hi, lo = left
    if transposed:
        pick = [w[pl.ds(n, BLOCK), :] for w in right]
        dims = (((1,), (1,)), ((), ()))
    else:
        pick = [w[:, pl.ds(n, BLOCK)] for w in right]
        dims = (((1,), (0,)), ((), ()))
    dot = functools.partial(lax.dot_general, dimension_numbers=dims, preferred_element_type=f32)
    upper = hi[...]
    return dot(upper, pick[0]) + dot(upper, pick[1]) + dot(lo[...], pick[0])


def layer(left, right, columns, transposed, finish, held, carry=0):
    steps = columns // BLOCK

    def body(k, carry):
        value = tile(left, right, pl.multiple_of(k * BLOCK, BLOCK), transposed)
        n = pl.multiple_of(jnp.maximum(k - 1, 0) * BLOCK, BLOCK)
        after = finish(n, held[...], carry)
        held[...] = value
        return jax.tree.map(lambda new, old: jnp.where(k > 0, new, old), after, carry)

    carry = lax.fori_loop(0, steps, body, carry)
    return finish((steps - 1) * BLOCK, held[...], carry)


def gated(gate, target):
    def finish(n, value, carry):
        upper, lower = halves_of(value * gate[:, pl.ds(n, BLOCK)].astype(f32))
        target[0][:, pl.ds(n, BLOCK)] = upper
        target[1][:, pl.ds(n, BLOCK)] = lower
        return carry

    return finish


def forward_kernel(
    with_sums, counts, own, other, gate_one, gate_two,
    in_hi, in_lo, mid_hi, mid_lo, out_hi, out_lo, cov_hi, cov_lo, *rest
):
    if with_sums:
        sums_in, z_hi, z_lo, sums = rest[:4]
    else:
        z_hi, z_lo = rest[:2]
    x_hi, x_lo, a_hi, a_lo, b_hi, b_lo, t_full, t_hi, t_lo, held = rest[-10:]
    rows = own.shape[0]
    for start, part in ((0, own), (WIDE, other)):
        upper, lower = halves_of(part[...])
        x_hi[:, start : start + WIDE] = upper
        x_lo[:, start : start + WIDE] = lower
    hidden = mid_hi.shape[0]
    channels = cov_hi.shape[0]
    layer((x_hi, x_lo), (in_hi, in_lo), hidden, False, gated(gate_one, (a_hi, a_lo)), held)
    layer((a_hi, a_lo), (mid_hi, mid_lo), hidden, False, gated(gate_two, (b_hi, b_lo)), held)

    def keep_outputs(n, value, carry):
        if with_sums:
            t_full[:, pl.ds(n, BLOCK)] = value
        upper, lower = halves_of(value)
        t_hi[:, pl.ds(n, BLOCK)] = upper
        t_lo[:, pl.ds(n, BLOCK)] = lower
        return carry

    layer((b_hi, b_lo), (out_hi, out_lo), channels, True, keep_outputs, held)
    live = lax.broadcasted_iota(jnp.int32, (rows, BLOCK), 0) < counts[0]

    def keep_weighted(n, value, carry):
        upper, lower = halves_of(value)
        z_hi[:, pl.ds(n, BLOCK)] = upper
        z_lo[:, pl.ds(n, BLOCK)] = lower
        if with_sums:
            carry = carry + folded(jnp.where(live, value * t_full[:, pl.ds(n, BLOCK)], 0.0))
        return carry

    total = jnp.zeros((8, BLOCK), f32)
    total = layer((t_hi, t_lo), (cov_hi, cov_lo), channels, False, keep_weighted, held, total)
    if with_sums:
        lane = lax.broadcasted_iota(jnp.int32, (8, 128), 1)
        sums[...] = jnp.where(lane == 3, jnp.sum(total), sums_in[...])


def backward_kernel(
    z_hi, z_lo, gate_one, gate_two, mid_hi, mid_lo, out_hi, out_lo, b_hi, b_lo, a_hi, a_lo, held
):
    hidden = mid_hi.shape[0]
    layer((z_hi, z_lo), (out_hi, out_lo), hidden, False, gated(gate_two, (a_hi, a_lo)), held)
    layer((a_hi, a_lo), (mid_hi, mid_lo), hidden, True, gated(gate_one, (b_hi, b_lo)), held)


def gradient_kernel(scale, b_hi, b_lo, in_hi, in_lo, own_grad, other_grad):
    for start in range(0, 2 * WIDE, BLOCK):
        value = tile((b_hi, b_lo), (in_hi, in_lo), start, True)
        for first, target in ((0, own_grad), (WIDE, other_grad)):
            low, top = max(start, first), min(start + BLOCK, first + WIDE)
            if low < top:
                target[:, low - first : top - first] = value[:, low - start : top - start] * scale


def forward_call(counts, own, other, gates, weights, sums):
    rows = own.shape[0]
    hidden, channels = weights[2].shape[0], weights[6].shape[0]
    with_sums = sums is not None
    out = [shape((rows, channels), bf16)] * 2 + [shape((8, 128))] * with_sums
    pair = lambda n: [pltpu.VMEM((rows, n), bf16)] * 2
    args = (counts, own, other, *gates, *weights) + ((sums,) if with_sums else ())
    return call(
        functools.partial(forward_kernel, with_sums),
        out,
        [smem] + [vmem] * (len(args) - 1),
        [vmem] * len(out),
        pair(2 * WIDE)
        + pair(hidden)
        + pair(hidden)
        + [pltpu.VMEM((rows, channels), f32)]
        + pair(channels)
        + [pltpu.VMEM((rows, BLOCK), f32)],
        16,
        13,
    )(*args)


def backward_call(z, gates, weights):
    rows = z[0].shape[0]
    hidden = weights[2].shape[0]
    args = (*z, *gates, *weights[2:6])
    return call(
        backward_kernel,
        [shape((rows, hidden), bf16)] * 2,
        [vmem] * len(args),
        [vmem] * 2,
        [pltpu.VMEM((rows, hidden), bf16)] * 2 + [pltpu.VMEM((rows, BLOCK), f32)],
        10,
        8,
    )(*args)


def gradient_call(scale, back, weights):
    rows = back[0].shape[0]
    return call(
        functools.partial(gradient_kernel, scale),
        [shape((rows, WIDE))] * 2,
        [vmem] * 4,
        [vmem] * 2,
        [],
        8,
        3,
    )(*back, *weights[:2])


def hot_rows(cell, cells):
    return (cell == cells).astype(f32).astype(bf16)


def merged(both):
    return both[:, :WIDE] + both[:, WIDE:]


def edge_kernel(
    counts, cells, own, other, coupling, columns, parts, south, north, west, east, *lines
):
    lats, lons, _ = coupling.shape
    slots = own.shape[0]
    width = west.shape[1]
    pieces = [(k, s) for s in range(0, slots, BLOCK) for k in range(2)]
    for b, (k, s) in enumerate(pieces):
        row = lax.broadcasted_iota(jnp.int32, (BLOCK, WIDE), 0) + s
        part = (own, other)[k][s : s + BLOCK, :]
        upper, lower = halves_of(jnp.where(row < counts[k], part, 0.0))
        parts[b, :, 0:WIDE] = upper
        parts[b, :, WIDE : 2 * WIDE] = lower
    total = 4 * lats + 4 * lons
    r = lax.broadcasted_iota(jnp.int32, (total, BLOCK), 0)
    cell = jnp.full_like(r, -1)
    start = 0
    spans = []
    for lon in (0, 1, lons - 2, lons - 1):
        inside = (r >= start) & (r < start + lats)
        cell = jnp.where(inside, (r - start) * lons + lon, cell)
        spans.append((start, lats))
        start += lats
    for lat in (0, 1, lats - 2, lats - 1):
        inside = (r >= start) & (r < start + lons)
        cell = jnp.where(inside, r - start + lat * lons, cell)
        spans.append((start, lons))
        start += lons
    value = jnp.zeros((total, 2 * WIDE), f32)
    for b in range(len(pieces)):
        hot = hot_rows(cell, cells[b : b + 1, :])
        value = value + jnp.dot(hot, parts[b], preferred_element_type=f32)
    value = merged(value)[:, :width]
    for line, (start, count) in zip(lines, spans):
        line[...] = value[start : start + count]
    west[...] = lines[0][...] * columns[:, 1:2]
    east[...] = lines[3][...] * columns[:, 0:1]
    south[0] = lines[4][...] * coupling[0][:, 3:4]
    north[0] = lines[7][...] * coupling[lats - 1][:, 2:3]


def edge_shapes(lats, lons, width):
    return [shape((1, lons, width))] * 2 + [shape((lats, width))] * 2


def edge_call(counts, cells, own, other, coupling, columns, width):
    lats, lons, _ = coupling.shape
    slots = own.shape[0]
    out = [shape((2 * slots // BLOCK, BLOCK, 2 * WIDE), bf16)] + edge_shapes(lats, lons, width)
    out += [shape((lats, width))] * 4 + [shape((lons, width))] * 4
    return call(edge_kernel, out, [smem] + [vmem] * 5, [vmem] * len(out), [], 12, 2)(
        counts, cells, own, other, coupling, columns
    )


def spread_kernel(counts, cells, parts, field):
    lats, lons, width = field.shape
    chunk = 256
    upper = [counts[k] > BLOCK for k in range(2)]

    def body(b, carry):
        cell = lax.broadcasted_iota(jnp.int32, (chunk, BLOCK), 0) + b * chunk
        lat = pl.ds(b * (chunk // lons), chunk // lons)

        def product(blocks):
            hot = [hot_rows(cell, cells[pl.ds(k, 1), :]) for k in blocks]
            part = [parts[k] for k in blocks]
            both = jnp.dot(
                jnp.concatenate(hot, axis=1),
                jnp.concatenate(part, axis=0),
                preferred_element_type=f32,
            )
            field[lat] = merged(both)[:, :width].reshape(chunk // lons, lons, width)

        @pl.when(upper[0] & upper[1])
        def _():
            product((0, 1, 2, 3))

        @pl.when(upper[0] != upper[1])
        def _():
            product((0, 1, jnp.where(upper[0], 2, 3)))

        @pl.when(jnp.logical_not(upper[0] | upper[1]))
        def _():
            product((0, 1))

        return carry

    lax.fori_loop(0, lats * lons // chunk, body, 0)


def spread_call(counts, cells, parts, lats, lons, width):
    return call(
        spread_kernel,
        [shape((lats, lons, width))],
        [smem] + [vmem] * 2,
        [vmem],
        [],
        8,
        4,
    )(counts, cells, parts)[0]


def border_kernel(
    south, north, west, east, w0, w1, e1, e0, s0, s1, n1, n0, coupling, columns, rates,
    out_south, out_north, out_west, out_east
):
    lats, width = w0.shape
    lons = s0.shape[0]
    rate = rates[...]
    lat = lax.broadcasted_iota(jnp.int32, (lats, width), 0)
    lon = lax.broadcasted_iota(jnp.int32, (lons, width), 0)

    def column(line, inner, halo, first, target, end):
        c = [columns[:, first + k : first + k + 1] for k in range(4)]
        value = line[...]
        flux = halo[...] + c[0] * inner[...]
        flux = flux + from_west(c[1] * value, south[0, end : end + 1, :], lat)
        flux = flux + from_east(c[2] * value, north[0, end : end + 1, :], lat)
        target[...] = value + rate * (flux - c[3] * value)

    column(w0, w1, west, 2, out_west, 0)
    column(e0, e1, east, 6, out_east, lons - 1)

    def along(i, line, flux):
        c = coupling[i]
        value = line[...]
        flux = flux + from_west(c[:, 0:1] * value, west[i : i + 1, :], lon)
        flux = flux + from_east(c[:, 1:2] * value, east[i : i + 1, :], lon)
        return value + rate * (flux - c[:, 4:5] * value)

    out_south[0] = along(0, s0, south[0] + coupling[1][:, 3:4] * s1[...])
    out_north[0] = along(lats - 1, n0, north[0] + coupling[lats - 2][:, 2:3] * n1[...])


def border_call(halo, lines, coupling, columns, rates):
    lats, width = lines[0].shape
    out = edge_shapes(lats, lines[4].shape[0], width)
    return call(border_kernel, out, [vmem] * 15, [vmem] * 4, [], 4, 1)(
        *halo, *lines, coupling, columns, rates
    )


def adjoint_rows(field, south, north, west, east, coupling, rates, finish, carry, after=None):
    lats, lons, width = field.shape
    rate = rates[...]
    lon = lax.broadcasted_iota(jnp.int32, (lons, width), 0)

    def row(i, below, above, carry):
        value = field[i]
        c = coupling[i]
        flux = below + above
        flux = flux + from_west(c[:, 0:1] * value, west[pl.ds(i, 1), :], lon)
        flux = flux + from_east(c[:, 1:2] * value, east[pl.ds(i, 1), :], lon)
        return finish(i, value + rate * (flux - c[:, 4:5] * value), carry)

    def below(i):
        return coupling[i - 1][:, 2:3] * field[i - 1]

    def above(i):
        return coupling[i + 1][:, 3:4] * field[i + 1]

    return sweep(lats, row, below, above, south[0], north[0], carry, after)


def basis_kernel(
    field, south, north, west, east, coupling, rates, right_side, sums_in, basis, sums
):
    _, _, width = field.shape

    def finish(i, value, carry):
        basis[i] = value
        return carry[0] + folded(right_side[i] * value), carry[1] + folded(value * value)

    zero = jnp.zeros((8, width), f32)
    cross, square = adjoint_rows(
        field, south, north, west, east, coupling, rates, finish, (zero, zero)
    )
    lane = lax.broadcasted_iota(jnp.int32, (8, 128), 1)
    result = jnp.where(lane == 1, jnp.sum(cross), sums_in[...])
    sums[...] = jnp.where(lane == 2, jnp.sum(square), result)


def basis_call(field, halo, coupling, rates, right_side, sums):
    out = [shape(field.shape), shape((8, 128))]
    return call(basis_kernel, out, [vmem] * 9, [vmem] * 2, [], 6, 5)(
        field, *halo, coupling, rates, right_side, sums
    )


def final_kernel(
    field, south, north, west, east, coupling, rates, right_side, basis, sums,
    solution_out, residual_out, solution_part, residual_part, sems
):
    lats, _, _ = field.shape
    s = sums[0:1, :]
    rr, rv, vv, vy = s[:, 0:1], s[:, 1:2], s[:, 2:3], s[:, 3:4]
    q = SCALE * rv
    den = rr + q
    first_step = rr / den
    p = SCALE * first_step
    rest = q / den
    new = p * p * vv - rest * rest * rr
    a = rest + new / rr
    square = a * a * rr - 2.0 * a * p * rv + p * p * vv
    curve = a * a * q - 2.0 * a * p * (SCALE * vv) + p * p * vy
    step = new / (square + curve)
    k_right = first_step + step * a
    k_basis = -(step * p)
    l_right = rest - step * a
    l_basis = step * p - p - step * a * SCALE
    l_image = step * p
    outs = ((solution_part, solution_out), (residual_part, residual_out))

    def finish(i, value, carry):
        solution_part[i] = k_right * right_side[i] + k_basis * basis[i]
        residual_part[i] = l_right * right_side[i] + l_basis * basis[i] + l_image * value
        return carry

    def start(g):
        rows = pl.ds(g * GROUP, GROUP)
        for k, (part, out) in enumerate(outs):
            pltpu.make_async_copy(part.at[rows], out.at[rows], sems.at[k]).start()

    def after(g):
        if not isinstance(g, int) or g > 0:
            start(g - 1)

    adjoint_rows(field, south, north, west, east, coupling, rates, finish, 0, after)
    start(lats // GROUP - 1)
    for k, (part, out) in enumerate(outs):
        pltpu.make_async_copy(part, out, sems.at[k]).wait()


def final_call(field, halo, coupling, rates, right_side, basis, sums):
    return call(
        final_kernel,
        [shape(field.shape)] * 2,
        [vmem] * 10,
        [hbm] * 2,
        [pltpu.VMEM(field.shape, f32)] * 2 + [pltpu.SemaphoreType.DMA((2,))],
        12,
        6,
    )(field, *halo, coupling, rates, right_side, basis, sums)


def shifted(value, axis, step):
    count = lax.axis_size(axis)
    return lax.ppermute(value, axis, [(i, (i + step) % count) for i in range(count)])


def exchanged(south_row, north_row, west_col, east_col):
    from_west = shifted(east_col, "col", 1)
    from_east = shifted(west_col, "col", -1)
    from_south = shifted(north_row, "row", 1)
    from_north = shifted(south_row, "row", -1)
    return from_south, from_north, from_west, from_east


def swapped(value):
    return lax.ppermute(value, "side", [(0, 1), (1, 0)])


def everyone(values):
    n = 4
    total = values + swapped(values)
    total = total + sum(shifted(total, "row", k) for k in range(1, n))
    size = lax.axis_size("col")
    for low in (True, False):
        base = total
        for k in range(1, n):
            if low:
                pairs = [(c, (c // n) * n + (c % n + k) % n) for c in range(size)]
            else:
                pairs = [(c, ((c // n + k) % n) * n + c % n) for c in range(size)]
            total = total + lax.ppermute(base, "col", pairs)
    return total


def local(
    right_side,
    couplings,
    channel_rates,
    weight_in,
    weight_mid,
    weight_out,
    inverse_cov,
    profile_cells,
    profile_counts,
    gate_first,
    gate_second,
):
    side_index = lax.axis_index("side")
    tile_count = lax.axis_size("row") * lax.axis_size("col")
    tile_index = lax.axis_index("row") * lax.axis_size("col") + lax.axis_index("col")
    lats, lons, width = right_side.shape
    halo = exchanged(
        right_side[:1], right_side[lats - 1 :], right_side[:, 0], right_side[:, lons - 1]
    )
    latitude = lax.axis_index("row") * lats + jnp.arange(lats)[None, :, None]
    plane = jnp.arange(4)[:, None, None]
    closed = (plane == 2) & (latitude == lats * lax.axis_size("row") - 1)
    closed = closed | ((plane == 3) & (latitude == 0))
    planes = jnp.where(closed, 0.0, couplings)
    planes = jnp.concatenate([planes, jnp.sum(planes, axis=0, keepdims=True)], axis=0)
    coupling = jnp.transpose(planes, (1, 2, 0))
    pick = ((0, lons - 1), (1, 0), (1, 1), (2, 0), (3, 0), (4, 0))
    pick += ((0, lons - 2), (2, lons - 1), (3, lons - 1), (4, lons - 1))
    columns = jnp.stack([planes[k][:, j] for k, j in pick], axis=1)
    rates = channel_rates[None, :]
    order = jnp.stack([side_index, 1 - side_index])
    cells = jnp.where(side_index == 0, profile_cells, profile_cells[::-1])
    cells = jnp.clip(cells, 0, lats * lons - 1)
    pieces = cells.reshape(2, -1, BLOCK).transpose(1, 0, 2).reshape(-1, BLOCK)
    counts = profile_counts[order * tile_count + tile_index]
    weights = prepare_call(
        order[:1], weight_in, weight_mid, weight_out.T, inverse_cov, 3 * BLOCK
    )
    gates = (gate_first, gate_second)

    own, other, sums = tangent_call(True, cells, counts, right_side, halo, coupling, rates)
    z = forward_call(counts, own, swapped(other), gates, weights, None)
    back = backward_call(z, gates, weights)
    own, other = gradient_call(1.0 / SCALE, back, weights)
    other = swapped(other)
    parts, *out = edge_call(counts, pieces, own, other, coupling, columns, width)
    halo = exchanged(*out[:4])
    field = spread_call(counts, pieces, parts, lats, lons, width)
    outer = border_call(halo, out[4:], coupling, columns, rates)
    outer = exchanged(*outer)
    basis, sums = basis_call(field, halo, coupling, rates, right_side, sums)
    own, other = tangent_call(False, cells, counts, basis, outer, coupling, rates)
    *z, sums = forward_call(counts, own, swapped(other), gates, weights, sums)
    sums = everyone(sums)
    back = backward_call(z, gates, weights)
    own, other = gradient_call(1.0, back, weights)
    other = swapped(other)
    parts, *out = edge_call(counts, pieces, own, other, coupling, columns, width)
    halo = exchanged(*out[:4])
    field = spread_call(counts, pieces, parts, lats, lons, width)
    return tuple(final_call(field, halo, coupling, rates, right_side, basis, sums))


def solution(mesh):
    in_specs = (
        P("row", "col", "side"),
        P(None, "row", "col"),
        P("side"),
        P(),
        P(),
        P(),
        P(),
        P(None, ("row", "col")),
        P(),
        P(("side", "row", "col"), None),
        P(("side", "row", "col"), None),
    )
    out_specs = (P("row", "col", "side"), P("row", "col", "side"))
    return jax.shard_map(local, mesh=mesh, in_specs=in_specs, out_specs=out_specs, check_vma=False)
```

```python
import functools

import jax
import jax.numpy as jnp
from jax import lax
from jax.experimental import pallas as pl
from jax.experimental.pallas import tpu as pltpu
from jax.sharding import PartitionSpec as P

SCALE = 2.0**40
BLOCK = 256
f32, bf16 = jnp.float32, jnp.bfloat16
vmem = pl.BlockSpec(memory_space=pltpu.VMEM)
smem = pl.BlockSpec(memory_space=pltpu.SMEM)
hbm = pl.BlockSpec(memory_space=pl.ANY)


WIDE = 384
GROUP = 4


def shape(dims, dtype=f32):
    return jax.ShapeDtypeStruct(dims, dtype)


def call(kernel, out, in_specs, out_specs, scratch, mib, micros):
    return pl.pallas_call(
        kernel,
        out_shape=out,
        in_specs=in_specs,
        out_specs=out_specs,
        scratch_shapes=scratch,
        compiler_params=pltpu.CompilerParams(vmem_limit_bytes=mib << 20),
        cost_estimate=pl.CostEstimate(
            flops=int(micros * 1e9), bytes_accessed=int(micros * 3e6), transcendentals=0
        ),
    )


def halves_of(value):
    upper = value.astype(bf16)
    return upper, (value - upper.astype(f32)).astype(bf16)


def folded(value):
    rows, width = value.shape
    return jnp.sum(value.reshape(rows // 8, 8, width), axis=0)


def lane_vector(scalars):
    lane = lax.broadcasted_iota(jnp.int32, (8, 128), 1)
    result = jnp.zeros((8, 128), f32)
    for k, value in enumerate(scalars):
        result = jnp.where(lane == k, value, result)
    return result


def from_west(value, west_row, lon):
    last = value.shape[0] - 1
    return jnp.where(lon == 0, west_row, jnp.concatenate([value[last:], value[:last]], axis=0))


def from_east(value, east_row, lon):
    last = value.shape[0] - 1
    return jnp.where(lon == last, east_row, jnp.concatenate([value[1:], value[:1]], axis=0))


def sweep(lats, row, below, above, south, north, carry, after=None):
    def group(g, low, high, carry):
        for k in range(GROUP):
            i = g * GROUP + k
            under = south if low and k == 0 else below(i)
            over = north if high and k == GROUP - 1 else above(i)
            carry = row(i, under, over, carry)
        if after is not None:
            after(g)
        return carry

    last = lats // GROUP - 1
    carry = group(0, True, False, carry)
    carry = lax.fori_loop(1, last, lambda g, c: group(g, False, False, c), carry)
    return group(last, False, True, carry)


def prepare_kernel(
    side, w_in, w_mid, w_out, cov, in_hi, in_lo, mid_hi, mid_lo, out_hi, out_lo, cov_hi, cov_lo
):
    for target in (in_hi, in_lo, out_hi, out_lo, cov_hi, cov_lo):
        target[...] = jnp.zeros_like(target)
    half = w_in.shape[0] // 2
    hidden = w_mid.shape[0]
    channels = cov.shape[0]

    def columns(total, step, move):
        def body(k, carry):
            move(pl.ds(pl.multiple_of(k * step, step), step))
            return carry

        lax.fori_loop(0, total // step, body, 0)
        if total % step:
            move(slice(total - total % step, total))

    for flag in range(2):

        @pl.when(side[0] == flag)
        def _(flag=flag):
            for target, source in ((0, flag * half), (WIDE, (1 - flag) * half)):

                def move(n, target=target, source=source):
                    upper, lower = halves_of(w_in[source : source + half, n])
                    in_hi[target : target + half, n] = upper
                    in_lo[target : target + half, n] = lower

                columns(hidden, 128, move)

    def move_cov(n):
        upper, lower = halves_of(cov[:, n])
        cov_hi[:channels, n] = upper
        cov_lo[:channels, n] = lower

    columns(channels, 128, move_cov)

    def move_out(n):
        upper, lower = halves_of(w_out[:, n])
        out_hi[:channels, n] = upper
        out_lo[:channels, n] = lower

    columns(hidden, 128, move_out)

    def move_mid(n):
        upper, lower = halves_of(w_mid[n, :])
        mid_hi[n, :] = upper
        mid_lo[n, :] = lower

    columns(hidden, 64, move_mid)


def prepare_call(side, w_in, w_mid, w_out, cov, channels):
    hidden = w_mid.shape[0]
    dims = [(2 * WIDE, hidden), (hidden, hidden), (channels, hidden), (channels, channels)]
    out = [shape(d, bf16) for d in dims for _ in range(2)]
    return call(
        prepare_kernel,
        out,
        [smem] + [vmem] * 4,
        [vmem] * 8,
        [],
        4,
        3,
    )(side, w_in, w_mid, w_out, cov)


def tangent_kernel(
    with_square, cells, counts, field, south, north, west, east, coupling, rates, own, other, *rest
):
    image = rest[-1]
    lats, lons, width = field.shape
    rate = rates[...]
    tail = width - 256
    lon = lax.broadcasted_iota(jnp.int32, (lons, width), 0)
    image[2] = jnp.zeros_like(image[2])

    def row(i, below, above, total):
        value = field[i]
        c = coupling[i]
        to_west = from_west(value, west[pl.ds(i, 1), :], lon)
        to_east = from_east(value, east[pl.ds(i, 1), :], lon)
        flux = c[:, 0:1] * (to_east - value)
        flux = flux + c[:, 1:2] * (to_west - value)
        flux = flux + c[:, 2:3] * (above - value)
        flux = flux + c[:, 3:4] * (below - value)
        result = value + rate * flux
        rows = pl.ds(i * lons if isinstance(i, int) else pl.multiple_of(i * lons, lons), lons)
        image[0, rows, :] = result[:, 0:128]
        image[1, rows, :] = result[:, 128:256]
        image[2, rows, 0:tail] = result[:, 256:]
        if with_square:
            total = total + folded(value * value)
        return total

    total = jnp.zeros((8, width), f32)
    total = sweep(
        lats, row, lambda i: field[i - 1], lambda i: field[i + 1], south[0], north[0], total
    )
    if with_square:
        rest[0][...] = lane_vector([jnp.sum(total)])

    place = lax.broadcasted_iota(jnp.int32, (8, 128), 0)

    def gather(which, out):
        def body(b, carry):
            first = pl.multiple_of(b * 8, 8)
            found = [cells[which, first + k] for k in range(8)]
            for t in range(3):
                block = image[t, pl.ds(found[0], 8, stride=0), :]
                for k in range(1, 8):
                    block = jnp.where(place == k, image[t, pl.ds(found[k], 8, stride=0), :], block)
                out[pl.ds(first, 8), t * 128 : (t + 1) * 128] = block
            return carry

        lax.fori_loop(0, (counts[which] + 7) // 8, body, 0)

    gather(1, other)
    gather(0, own)


def tangent_call(with_square, cells, counts, field, halo, coupling, rates):
    lats, lons, _ = field.shape
    slots = cells.shape[1]
    out = [shape((slots, WIDE))] * 2 + [shape((8, 128))] * with_square
    return call(
        functools.partial(tangent_kernel, with_square),
        out,
        [smem, smem] + [vmem] * 7,
        [vmem] * len(out),
        [pltpu.VMEM((3, lats * lons, 128), f32)],
        8,
        6,
    )(cells, counts, field, *halo, coupling, rates)


def tile(left, right, n, transposed):
    hi, lo = left
    if transposed:
        pick = [w[pl.ds(n, BLOCK), :] for w in right]
        dims = (((1,), (1,)), ((), ()))
    else:
        pick = [w[:, pl.ds(n, BLOCK)] for w in right]
        dims = (((1,), (0,)), ((), ()))
    dot = functools.partial(lax.dot_general, dimension_numbers=dims, preferred_element_type=f32)
    upper = hi[...]
    return dot(upper, pick[0]) + dot(upper, pick[1]) + dot(lo[...], pick[0])


def layer(left, right, columns, transposed, finish, held, carry=0):
    steps = columns // BLOCK

    def body(k, carry):
        value = tile(left, right, pl.multiple_of(k * BLOCK, BLOCK), transposed)
        n = pl.multiple_of(jnp.maximum(k - 1, 0) * BLOCK, BLOCK)
        after = finish(n, held[...], carry)
        held[...] = value
        return jax.tree.map(lambda new, old: jnp.where(k > 0, new, old), after, carry)

    carry = lax.fori_loop(0, steps, body, carry)
    return finish((steps - 1) * BLOCK, held[...], carry)


def gated(gate, target):
    def finish(n, value, carry):
        upper, lower = halves_of(value * gate[:, pl.ds(n, BLOCK)].astype(f32))
        target[0][:, pl.ds(n, BLOCK)] = upper
        target[1][:, pl.ds(n, BLOCK)] = lower
        return carry

    return finish


def forward_kernel(
    with_sums, counts, own, other, gate_one, gate_two,
    in_hi, in_lo, mid_hi, mid_lo, out_hi, out_lo, cov_hi, cov_lo, *rest
):
    if with_sums:
        sums_in, z_hi, z_lo, sums = rest[:4]
    else:
        z_hi, z_lo = rest[:2]
    x_hi, x_lo, a_hi, a_lo, b_hi, b_lo, t_full, t_hi, t_lo, held = rest[-10:]
    rows = own.shape[0]
    for start, part in ((0, own), (WIDE, other)):
        upper, lower = halves_of(part[...])
        x_hi[:, start : start + WIDE] = upper
        x_lo[:, start : start + WIDE] = lower
    hidden = mid_hi.shape[0]
    channels = cov_hi.shape[0]
    layer((x_hi, x_lo), (in_hi, in_lo), hidden, False, gated(gate_one, (a_hi, a_lo)), held)
    layer((a_hi, a_lo), (mid_hi, mid_lo), hidden, False, gated(gate_two, (b_hi, b_lo)), held)

    def keep_outputs(n, value, carry):
        if with_sums:
            t_full[:, pl.ds(n, BLOCK)] = value
        upper, lower = halves_of(value)
        t_hi[:, pl.ds(n, BLOCK)] = upper
        t_lo[:, pl.ds(n, BLOCK)] = lower
        return carry

    layer((b_hi, b_lo), (out_hi, out_lo), channels, True, keep_outputs, held)
    live = lax.broadcasted_iota(jnp.int32, (rows, BLOCK), 0) < counts[0]

    def keep_weighted(n, value, carry):
        upper, lower = halves_of(value)
        z_hi[:, pl.ds(n, BLOCK)] = upper
        z_lo[:, pl.ds(n, BLOCK)] = lower
        if with_sums:
            carry = carry + folded(jnp.where(live, value * t_full[:, pl.ds(n, BLOCK)], 0.0))
        return carry

    total = jnp.zeros((8, BLOCK), f32)
    total = layer((t_hi, t_lo), (cov_hi, cov_lo), channels, False, keep_weighted, held, total)
    if with_sums:
        lane = lax.broadcasted_iota(jnp.int32, (8, 128), 1)
        sums[...] = jnp.where(lane == 3, jnp.sum(total), sums_in[...])


def backward_kernel(
    z_hi, z_lo, gate_one, gate_two, mid_hi, mid_lo, out_hi, out_lo, b_hi, b_lo, a_hi, a_lo, held
):
    hidden = mid_hi.shape[0]
    layer((z_hi, z_lo), (out_hi, out_lo), hidden, False, gated(gate_two, (a_hi, a_lo)), held)
    layer((a_hi, a_lo), (mid_hi, mid_lo), hidden, True, gated(gate_one, (b_hi, b_lo)), held)


def gradient_kernel(scale, b_hi, b_lo, in_hi, in_lo, own_grad, other_grad):
    for start in range(0, 2 * WIDE, BLOCK):
        value = tile((b_hi, b_lo), (in_hi, in_lo), start, True)
        for first, target in ((0, own_grad), (WIDE, other_grad)):
            low, top = max(start, first), min(start + BLOCK, first + WIDE)
            if low < top:
                target[:, low - first : top - first] = value[:, low - start : top - start] * scale


def forward_call(counts, own, other, gates, weights, sums):
    rows = own.shape[0]
    hidden, channels = weights[2].shape[0], weights[6].shape[0]
    with_sums = sums is not None
    out = [shape((rows, channels), bf16)] * 2 + [shape((8, 128))] * with_sums
    pair = lambda n: [pltpu.VMEM((rows, n), bf16)] * 2
    args = (counts, own, other, *gates, *weights) + ((sums,) if with_sums else ())
    return call(
        functools.partial(forward_kernel, with_sums),
        out,
        [smem] + [vmem] * (len(args) - 1),
        [vmem] * len(out),
        pair(2 * WIDE)
        + pair(hidden)
        + pair(hidden)
        + [pltpu.VMEM((rows, channels), f32)]
        + pair(channels)
        + [pltpu.VMEM((rows, BLOCK), f32)],
        16,
        13,
    )(*args)


def backward_call(z, gates, weights):
    rows = z[0].shape[0]
    hidden = weights[2].shape[0]
    args = (*z, *gates, *weights[2:6])
    return call(
        backward_kernel,
        [shape((rows, hidden), bf16)] * 2,
        [vmem] * len(args),
        [vmem] * 2,
        [pltpu.VMEM((rows, hidden), bf16)] * 2 + [pltpu.VMEM((rows, BLOCK), f32)],
        10,
        8,
    )(*args)


def gradient_call(scale, back, weights):
    rows = back[0].shape[0]
    return call(
        functools.partial(gradient_kernel, scale),
        [shape((rows, WIDE))] * 2,
        [vmem] * 4,
        [vmem] * 2,
        [],
        8,
        3,
    )(*back, *weights[:2])


def hot_rows(cell, cells):
    return (cell == cells).astype(f32).astype(bf16)


def merged(both):
    return both[:, :WIDE] + both[:, WIDE:]


def edge_kernel(
    counts, cells, own, other, coupling, columns, parts, south, north, west, east, *lines
):
    lats, lons, _ = coupling.shape
    slots = own.shape[0]
    width = west.shape[1]
    pieces = [(k, s) for s in range(0, slots, BLOCK) for k in range(2)]
    for b, (k, s) in enumerate(pieces):
        row = lax.broadcasted_iota(jnp.int32, (BLOCK, WIDE), 0) + s
        part = (own, other)[k][s : s + BLOCK, :]
        upper, lower = halves_of(jnp.where(row < counts[k], part, 0.0))
        parts[b, :, 0:WIDE] = upper
        parts[b, :, WIDE : 2 * WIDE] = lower
    total = 4 * lats + 4 * lons
    r = lax.broadcasted_iota(jnp.int32, (total, BLOCK), 0)
    cell = jnp.full_like(r, -1)
    start = 0
    spans = []
    for lon in (0, 1, lons - 2, lons - 1):
        inside = (r >= start) & (r < start + lats)
        cell = jnp.where(inside, (r - start) * lons + lon, cell)
        spans.append((start, lats))
        start += lats
    for lat in (0, 1, lats - 2, lats - 1):
        inside = (r >= start) & (r < start + lons)
        cell = jnp.where(inside, r - start + lat * lons, cell)
        spans.append((start, lons))
        start += lons
    value = jnp.zeros((total, 2 * WIDE), f32)
    for b in range(len(pieces)):
        hot = hot_rows(cell, cells[b : b + 1, :])
        value = value + jnp.dot(hot, parts[b], preferred_element_type=f32)
    value = merged(value)[:, :width]
    for line, (start, count) in zip(lines, spans):
        line[...] = value[start : start + count]
    west[...] = lines[0][...] * columns[:, 1:2]
    east[...] = lines[3][...] * columns[:, 0:1]
    south[0] = lines[4][...] * coupling[0][:, 3:4]
    north[0] = lines[7][...] * coupling[lats - 1][:, 2:3]


def edge_shapes(lats, lons, width):
    return [shape((1, lons, width))] * 2 + [shape((lats, width))] * 2


def edge_call(counts, cells, own, other, coupling, columns, width):
    lats, lons, _ = coupling.shape
    slots = own.shape[0]
    out = [shape((2 * slots // BLOCK, BLOCK, 2 * WIDE), bf16)] + edge_shapes(lats, lons, width)
    out += [shape((lats, width))] * 4 + [shape((lons, width))] * 4
    return call(edge_kernel, out, [smem] + [vmem] * 5, [vmem] * len(out), [], 12, 2)(
        counts, cells, own, other, coupling, columns
    )


def spread_kernel(counts, cells, parts, field):
    lats, lons, width = field.shape
    chunk = 256
    upper = [counts[k] > BLOCK for k in range(2)]

    def body(b, carry):
        cell = lax.broadcasted_iota(jnp.int32, (chunk, BLOCK), 0) + b * chunk
        lat = pl.ds(b * (chunk // lons), chunk // lons)

        def product(blocks):
            hot = [hot_rows(cell, cells[pl.ds(k, 1), :]) for k in blocks]
            part = [parts[k] for k in blocks]
            both = jnp.dot(
                jnp.concatenate(hot, axis=1),
                jnp.concatenate(part, axis=0),
                preferred_element_type=f32,
            )
            field[lat] = merged(both)[:, :width].reshape(chunk // lons, lons, width)

        @pl.when(upper[0] & upper[1])
        def _():
            product((0, 1, 2, 3))

        @pl.when(upper[0] != upper[1])
        def _():
            product((0, 1, jnp.where(upper[0], 2, 3)))

        @pl.when(jnp.logical_not(upper[0] | upper[1]))
        def _():
            product((0, 1))

        return carry

    lax.fori_loop(0, lats * lons // chunk, body, 0)


def spread_call(counts, cells, parts, lats, lons, width):
    return call(
        spread_kernel,
        [shape((lats, lons, width))],
        [smem] + [vmem] * 2,
        [vmem],
        [],
        8,
        4,
    )(counts, cells, parts)[0]


def border_kernel(
    south, north, west, east, w0, w1, e1, e0, s0, s1, n1, n0, coupling, columns, rates,
    out_south, out_north, out_west, out_east
):
    lats, width = w0.shape
    lons = s0.shape[0]
    rate = rates[...]
    lat = lax.broadcasted_iota(jnp.int32, (lats, width), 0)
    lon = lax.broadcasted_iota(jnp.int32, (lons, width), 0)

    def column(line, inner, halo, first, target, end):
        c = [columns[:, first + k : first + k + 1] for k in range(4)]
        value = line[...]
        flux = halo[...] + c[0] * inner[...]
        flux = flux + from_west(c[1] * value, south[0, end : end + 1, :], lat)
        flux = flux + from_east(c[2] * value, north[0, end : end + 1, :], lat)
        target[...] = value + rate * (flux - c[3] * value)

    column(w0, w1, west, 2, out_west, 0)
    column(e0, e1, east, 6, out_east, lons - 1)

    def along(i, line, flux):
        c = coupling[i]
        value = line[...]
        flux = flux + from_west(c[:, 0:1] * value, west[i : i + 1, :], lon)
        flux = flux + from_east(c[:, 1:2] * value, east[i : i + 1, :], lon)
        return value + rate * (flux - c[:, 4:5] * value)

    out_south[0] = along(0, s0, south[0] + coupling[1][:, 3:4] * s1[...])
    out_north[0] = along(lats - 1, n0, north[0] + coupling[lats - 2][:, 2:3] * n1[...])


def border_call(halo, lines, coupling, columns, rates):
    lats, width = lines[0].shape
    out = edge_shapes(lats, lines[4].shape[0], width)
    return call(border_kernel, out, [vmem] * 15, [vmem] * 4, [], 4, 1)(
        *halo, *lines, coupling, columns, rates
    )


def adjoint_rows(field, south, north, west, east, coupling, rates, finish, carry, after=None):
    lats, lons, width = field.shape
    rate = rates[...]
    lon = lax.broadcasted_iota(jnp.int32, (lons, width), 0)

    def row(i, below, above, carry):
        value = field[i]
        c = coupling[i]
        flux = below + above
        flux = flux + from_west(c[:, 0:1] * value, west[pl.ds(i, 1), :], lon)
        flux = flux + from_east(c[:, 1:2] * value, east[pl.ds(i, 1), :], lon)
        return finish(i, value + rate * (flux - c[:, 4:5] * value), carry)

    def below(i):
        return coupling[i - 1][:, 2:3] * field[i - 1]

    def above(i):
        return coupling[i + 1][:, 3:4] * field[i + 1]

    return sweep(lats, row, below, above, south[0], north[0], carry, after)


def basis_kernel(
    field, south, north, west, east, coupling, rates, right_side, sums_in, basis, sums
):
    _, _, width = field.shape

    def finish(i, value, carry):
        basis[i] = value
        return carry[0] + folded(right_side[i] * value), carry[1] + folded(value * value)

    zero = jnp.zeros((8, width), f32)
    cross, square = adjoint_rows(
        field, south, north, west, east, coupling, rates, finish, (zero, zero)
    )
    lane = lax.broadcasted_iota(jnp.int32, (8, 128), 1)
    result = jnp.where(lane == 1, jnp.sum(cross), sums_in[...])
    sums[...] = jnp.where(lane == 2, jnp.sum(square), result)


def basis_call(field, halo, coupling, rates, right_side, sums):
    out = [shape(field.shape), shape((8, 128))]
    return call(basis_kernel, out, [vmem] * 9, [vmem] * 2, [], 6, 5)(
        field, *halo, coupling, rates, right_side, sums
    )


def final_kernel(
    field, south, north, west, east, coupling, rates, right_side, basis, sums,
    solution_out, residual_out, solution_part, residual_part, sems
):
    lats, _, _ = field.shape
    s = sums[0:1, :]
    rr, rv, vv, vy = s[:, 0:1], s[:, 1:2], s[:, 2:3], s[:, 3:4]
    q = SCALE * rv
    den = rr + q
    first_step = rr / den
    p = SCALE * first_step
    rest = q / den
    new = p * p * vv - rest * rest * rr
    a = rest + new / rr
    square = a * a * rr - 2.0 * a * p * rv + p * p * vv
    curve = a * a * q - 2.0 * a * p * (SCALE * vv) + p * p * vy
    step = new / (square + curve)
    k_right = first_step + step * a
    k_basis = -(step * p)
    l_right = rest - step * a
    l_basis = step * p - p - step * a * SCALE
    l_image = step * p
    outs = ((solution_part, solution_out), (residual_part, residual_out))

    def finish(i, value, carry):
        solution_part[i] = k_right * right_side[i] + k_basis * basis[i]
        residual_part[i] = l_right * right_side[i] + l_basis * basis[i] + l_image * value
        return carry

    def start(g):
        rows = pl.ds(g * GROUP, GROUP)
        for k, (part, out) in enumerate(outs):
            pltpu.make_async_copy(part.at[rows], out.at[rows], sems.at[k]).start()

    def after(g):
        if not isinstance(g, int) or g > 0:
            start(g - 1)

    adjoint_rows(field, south, north, west, east, coupling, rates, finish, 0, after)
    start(lats // GROUP - 1)
    for k, (part, out) in enumerate(outs):
        pltpu.make_async_copy(part, out, sems.at[k]).wait()


def final_call(field, halo, coupling, rates, right_side, basis, sums):
    return call(
        final_kernel,
        [shape(field.shape)] * 2,
        [vmem] * 10,
        [hbm] * 2,
        [pltpu.VMEM(field.shape, f32)] * 2 + [pltpu.SemaphoreType.DMA((2,))],
        12,
        6,
    )(field, *halo, coupling, rates, right_side, basis, sums)


def shifted(value, axis, step):
    count = lax.axis_size(axis)
    return lax.ppermute(value, axis, [(i, (i + step) % count) for i in range(count)])


def exchanged(south_row, north_row, west_col, east_col):
    from_west = shifted(east_col, "col", 1)
    from_east = shifted(west_col, "col", -1)
    from_south = shifted(north_row, "row", 1)
    from_north = shifted(south_row, "row", -1)
    return from_south, from_north, from_west, from_east


def swapped(value):
    return lax.ppermute(value, "side", [(0, 1), (1, 0)])


def everyone(values):
    n = 4
    total = values + swapped(values)
    total = total + sum(shifted(total, "row", k) for k in range(1, n))
    size = lax.axis_size("col")
    for low in (True, False):
        base = total
        for k in range(1, n):
            if low:
                pairs = [(c, (c // n) * n + (c % n + k) % n) for c in range(size)]
            else:
                pairs = [(c, ((c // n + k) % n) * n + c % n) for c in range(size)]
            total = total + lax.ppermute(base, "col", pairs)
    return total


def local(
    right_side,
    couplings,
    channel_rates,
    weight_in,
    weight_mid,
    weight_out,
    inverse_cov,
    profile_cells,
    profile_counts,
    gate_first,
    gate_second,
):
    side_index = lax.axis_index("side")
    tile_count = lax.axis_size("row") * lax.axis_size("col")
    tile_index = lax.axis_index("row") * lax.axis_size("col") + lax.axis_index("col")
    lats, lons, width = right_side.shape
    halo = exchanged(
        right_side[:1], right_side[lats - 1 :], right_side[:, 0], right_side[:, lons - 1]
    )
    latitude = lax.axis_index("row") * lats + jnp.arange(lats)
    north_open = (latitude < lats * lax.axis_size("row") - 1)[:, None]
    south_open = (latitude > 0)[:, None]
    planes = [
        couplings[0],
        couplings[1],
        jnp.where(north_open, couplings[2], 0.0),
        jnp.where(south_open, couplings[3], 0.0),
    ]
    planes.append(planes[0] + planes[1] + planes[2] + planes[3])
    coupling = jnp.stack(planes, axis=2)
    pick = ((0, lons - 1), (1, 0), (1, 1), (2, 0), (3, 0), (4, 0))
    pick += ((0, lons - 2), (2, lons - 1), (3, lons - 1), (4, lons - 1))
    columns = jnp.stack([planes[k][:, j] for k, j in pick], axis=1)
    rates = channel_rates[None, :]
    order = jnp.stack([side_index, 1 - side_index])
    cells = jnp.clip(profile_cells[order], 0, lats * lons - 1)
    pieces = jnp.concatenate([cells[:, k : k + BLOCK] for k in range(0, cells.shape[1], BLOCK)], axis=0)
    counts = profile_counts[order * tile_count + tile_index]
    weights = prepare_call(
        order[:1], weight_in, weight_mid, weight_out.T, inverse_cov, 3 * BLOCK
    )
    gates = (gate_first, gate_second)

    own, other, sums = tangent_call(True, cells, counts, right_side, halo, coupling, rates)
    z = forward_call(counts, own, swapped(other), gates, weights, None)
    back = backward_call(z, gates, weights)
    own, other = gradient_call(1.0 / SCALE, back, weights)
    other = swapped(other)
    parts, *out = edge_call(counts, pieces, own, other, coupling, columns, width)
    halo = exchanged(*out[:4])
    field = spread_call(counts, pieces, parts, lats, lons, width)
    outer = border_call(halo, out[4:], coupling, columns, rates)
    outer = exchanged(*outer)
    basis, sums = basis_call(field, halo, coupling, rates, right_side, sums)
    own, other = tangent_call(False, cells, counts, basis, outer, coupling, rates)
    *z, sums = forward_call(counts, own, swapped(other), gates, weights, sums)
    sums = everyone(sums)
    back = backward_call(z, gates, weights)
    own, other = gradient_call(1.0, back, weights)
    other = swapped(other)
    parts, *out = edge_call(counts, pieces, own, other, coupling, columns, width)
    halo = exchanged(*out[:4])
    field = spread_call(counts, pieces, parts, lats, lons, width)
    return tuple(final_call(field, halo, coupling, rates, right_side, basis, sums))


def solution(mesh):
    in_specs = (
        P("row", "col", "side"),
        P(None, "row", "col"),
        P("side"),
        P(),
        P(),
        P(),
        P(),
        P(None, ("row", "col")),
        P(),
        P(("side", "row", "col"), None),
        P(("side", "row", "col"), None),
    )
    out_specs = (P("row", "col", "side"), P("row", "col", "side"))
    return jax.shard_map(local, mesh=mesh, in_specs=in_specs, out_specs=out_specs, check_vma=False)
```
